512 devices in a mesh: kv: 8 (over x, core), pool: 64 (over y, z).
Axes of the slice: x: 4, y: 4, z: 16, core: 2. Of those that a mesh axis runs over, the one named last changes fastest.
Arguments:
- hidden: bfloat16 [64, 2048], P('pool'), may hold values from -6 to 6
- norm_attn: bfloat16 [2048], replicated, may hold values from 0.099609375 to 1.8984375
- wq: bfloat16 [2048, 2048], P(None, 'kv'), may hold values from -0.125 to 0.125
- wkv: bfloat16 [2, 2048, 1024], P(None, None, 'kv'), may hold values from -0.125 to 0.125
- wo: bfloat16 [2048, 2048], P('kv'), may hold values from -0.125 to 0.125
- cache: bfloat16 [2, 1024, 128, 1024], P(None, 'pool', None, 'kv'), may hold values from -70 to 70, as said below
- slot_entry: int32 [1024], P('pool'), may hold values from -1 to 4095, as said below
- lengths: int32 [64], replicated, may hold values from 1 to 8192, as said below
- norm_mlp: bfloat16 [2048], replicated, may hold values from 0.099609375 to 1.8984375
- w_gate: bfloat16 [2048, 8192], P('pool', 'kv'), may hold values from -0.125 to 0.125
- w_up: bfloat16 [2048, 8192], P('pool', 'kv'), may hold values from -0.125 to 0.125
- w_down: bfloat16 [8192, 2048], P('kv', 'pool'), may hold values from -0.0625 to 0.0625
Outputs:
- output: bfloat16 [64, 2048], P('pool')
The draws below stay inside these ranges and needn't reach their ends.
Inputs may be any that keep to these rules, and one draw needn't show every extreme that they name: slot_entry[s] is -1 for a free slot, else r * 64 + b: the slot holds block b of request r, that is its cached positions b * 128 to b * 128 + 127 that lie below lengths[r]. Every block of every request below ceil(lengths[r] / 128) sits in exactly one slot, anywhere in the pool; a holder's slots are its 16 entries. Its new token stands at position lengths[r]. `cache`: keys and values of the cached tokens, already rotated.
All inputs are finite; a program needn't handle non-finite values.
Results may differ from the reference program's by a relative error of at most 0.012.
The reference program's roundings to bfloat16 on the way count: a program that leaves them out, or rounds other values in their place, can miss the bound.
Values may be sent and summed in bfloat16 or wider, within the bound.
A program may use at most 64 MiB of HBM per device.

```python
import math
import jax
import jax.numpy as jnp
from jax import lax

MODEL_WIDTH = 2048
QUERY_HEAD_COUNT = 16
KEY_VALUE_HEADS = 8
HEAD_SIZE = 128
FF = 8192
BLOCK_TOKENS = 128
HOLDER_SLOTS = 16
REQS = 64
MAXB = 64
N_POOL = 64


def page_plan(key):
    keys_all = jax.random.split(jax.random.fold_in(key, 7), 5)
    total_slots = N_POOL * HOLDER_SLOTS
    counts = jax.random.randint(keys_all[0], (REQS,), 1, 4, dtype=jnp.int32)
    chosen = jax.random.permutation(keys_all[1], REQS)[:3].astype(jnp.int32)
    longest = jnp.concatenate([chosen, jnp.array([REQS - 1], dtype=jnp.int32)])
    counts = counts.at[longest].set(MAXB)
    tail_tokens = jax.random.randint(keys_all[2], (REQS,), 1, BLOCK_TOKENS + 1, dtype=jnp.int32)
    tail_tokens = tail_tokens.at[REQS - 1].set(BLOCK_TOKENS)
    request_lengths = (counts - 1) * BLOCK_TOKENS + tail_tokens
    holder_weight = jax.random.randint(keys_all[3], (N_POOL,), 1, 5, dtype=jnp.int32)
    slot_score = jax.random.randint(keys_all[4], (total_slots,), 0, 4096, dtype=jnp.int32) * jnp.repeat(holder_weight, HOLDER_SLOTS)
    slot_score = slot_score * total_slots + jnp.arange(total_slots, dtype=jnp.int32)
    slot_order = jnp.argsort(slot_score)
    starts = jnp.cumsum(counts) - counts
    rank_index = jnp.arange(total_slots, dtype=jnp.int32)
    owners = jnp.sum((starts[None, :] <= rank_index[:, None]).astype(jnp.int32), axis=1) - 1
    used_count = jnp.sum(counts)
    entries = jnp.where(rank_index < used_count, owners * MAXB + rank_index - starts[owners], -1)
    slot_entry = jnp.zeros((total_slots,), jnp.int32).at[slot_order].set(entries.astype(jnp.int32))
    return (slot_entry, request_lengths.astype(jnp.int32))


def draw_slot_entry(key, part):
    return page_plan(key)[0]


def draw_lengths(key, part):
    return page_plan(key)[1]


def draw_cache(key, part):
    keys_all = jax.random.split(jax.random.fold_in(key, 11), 4)
    pooled_shape = (N_POOL * HOLDER_SLOTS, BLOCK_TOKENS, KEY_VALUE_HEADS * HEAD_SIZE)
    key_part = jnp.clip(jax.random.normal(keys_all[0], pooled_shape, jnp.float32), -6.0, 6.0)
    value_part = jnp.clip(jax.random.normal(keys_all[3], pooled_shape, jnp.float32), -6.0, 6.0)
    return jnp.stack([key_part, value_part]).astype(jnp.bfloat16)


def block_scale(own_key, extent, cuts, smallest, largest):
    def one(dim, shards_of):
        steps = jax.random.uniform(jax.random.fold_in(jax.random.fold_in(own_key, 6), dim), (shards_of,), jnp.float32, smallest / len(cuts), largest / len(cuts))
        return jnp.repeat(jnp.exp(steps), extent[dim] // shards_of).reshape((-1,) + (1,) * (len(extent) - dim - 1))

    gain = one(*cuts[0])
    for cut in cuts[1:]:
        gain = gain * one(*cut)
    return gain


def gaussian(own_key, dims, deviation, reach, shards=(), kind=jnp.bfloat16):
    factor_of = block_scale(own_key, dims, shards, -0.22, 0.18) if shards else 1.0
    result = jax.random.normal(own_key, dims, jnp.float32) * deviation * factor_of
    return jnp.minimum(jnp.maximum(result, -reach), reach).astype(kind)


def setup_inputs(seed: int = 0) -> dict:
    key_of = jax.random.split(jax.random.key(seed), 13)
    return {
        "hidden": gaussian(key_of[0], (REQS, MODEL_WIDTH), 1.0, 6.0, ((0, 64),)),
        "norm_attn": jnp.clip(1.0 + 0.18 * jax.random.normal(key_of[1], (MODEL_WIDTH,), jnp.float32), 0.099609375, 1.8984375).astype(jnp.bfloat16),
        "wq": gaussian(key_of[2], (MODEL_WIDTH, QUERY_HEAD_COUNT * HEAD_SIZE), MODEL_WIDTH ** -0.5, 0.125, ((1, 8),)),
        "wkv": gaussian(key_of[3], (2, MODEL_WIDTH, KEY_VALUE_HEADS * HEAD_SIZE), MODEL_WIDTH ** -0.5, 0.125, ((2, 8),)),
        "wo": gaussian(key_of[4], (QUERY_HEAD_COUNT * HEAD_SIZE, MODEL_WIDTH), (QUERY_HEAD_COUNT * HEAD_SIZE) ** -0.5, 0.125, ((0, 8),)),
        "cache": draw_cache(jax.random.fold_in(key_of[12], 71), 0),
        "slot_entry": draw_slot_entry(jax.random.fold_in(key_of[12], 71), 0),
        "lengths": draw_lengths(jax.random.fold_in(key_of[12], 71), 0),
        "norm_mlp": jnp.clip(1.0 + 0.18 * jax.random.normal(key_of[8], (MODEL_WIDTH,), jnp.float32), 0.099609375, 1.8984375).astype(jnp.bfloat16),
        "w_gate": gaussian(key_of[9], (MODEL_WIDTH, FF), MODEL_WIDTH ** -0.5, 0.125, ((0, 64), (1, 8))),
        "w_up": gaussian(key_of[10], (MODEL_WIDTH, FF), MODEL_WIDTH ** -0.5, 0.125, ((0, 64), (1, 8))),
        "w_down": gaussian(key_of[11], (FF, MODEL_WIDTH), FF ** -0.5, 0.0625, ((0, 8), (1, 64))),
    }


NEGATIVE = -1e+30
EPSILON = 1e-05
ROPE_BASE = 1000000.0

def narrow_rows(tensor):
    return lax.optimization_barrier(tensor.astype(jnp.bfloat16))

def rms_scale(inputs, gain_vec):
    widened = inputs.astype(jnp.float32)
    mean_square = lax.optimization_barrier(jnp.mean(widened * widened, axis=-1, keepdims=True))
    return narrow_rows(widened * lax.rsqrt(mean_square + EPSILON) * gain_vec.astype(jnp.float32))

def rotate(vectors, positions):
    head_width = vectors.shape[-1]
    halfway = head_width // 2
    frequency = jnp.exp(jnp.arange(halfway, dtype=jnp.float32) * (-2.0 * math.log(ROPE_BASE) / head_width))
    angles = positions.astype(jnp.float32)[:, None] * frequency[None, :]
    cosine = jnp.cos(angles)[:, None, :]
    sine_of = jnp.sin(angles)[:, None, :]
    leading = vectors[..., :halfway]
    trailing = vectors[..., halfway:]
    return jnp.concatenate([leading * cosine - trailing * sine_of, trailing * cosine + leading * sine_of], axis=-1)

def holder_terms(holder, grouped_queries, cache, slot_entry, lengths):
    first_slot = (holder * HOLDER_SLOTS).astype(jnp.int32)
    entries = lax.dynamic_slice_in_dim(slot_entry, first_slot, HOLDER_SLOTS)
    block_list = lax.dynamic_slice_in_dim(cache, first_slot, HOLDER_SLOTS, 1).astype(jnp.float32)
    live_slot = entries >= 0
    owners = jnp.where(live_slot, entries // MAXB, 0)
    block_index = jnp.where(live_slot, entries % MAXB, 0)
    picked = grouped_queries[owners].astype(jnp.float32)
    block_keys = block_list[0].reshape(HOLDER_SLOTS, BLOCK_TOKENS, KEY_VALUE_HEADS, HEAD_SIZE)
    block_values = block_list[1].reshape(HOLDER_SLOTS, BLOCK_TOKENS, KEY_VALUE_HEADS, HEAD_SIZE)
    scores = jnp.einsum('sgjd,stgd->sgjt', picked, block_keys)
    position = block_index[:, None] * BLOCK_TOKENS + jnp.arange(BLOCK_TOKENS, dtype=jnp.int32)[None, :]
    in_range = live_slot[:, None] & (position < lengths[owners][:, None])
    scores = jnp.where(in_range[:, None, None, :], scores, NEGATIVE)
    block_max = lax.optimization_barrier(jnp.max(scores, axis=-1))
    same_owner = (owners[:, None] == owners[None, :]) & live_slot[:, None] & live_slot[None, :]
    holder_max = lax.optimization_barrier(jnp.max(jnp.where(same_owner[:, :, None, None], block_max[None], NEGATIVE), axis=1))
    raised = jnp.where(in_range[:, None, None, :], jnp.exp(scores - holder_max[..., None]), 0.0)
    holder_total = lax.optimization_barrier(jnp.sum(raised, axis=-1))
    rounded = narrow_rows(raised).astype(jnp.float32)
    holder_output = jnp.einsum('sgjt,stgd->sgjd', rounded, block_values)
    return (holder_max, holder_total, holder_output)

def reference(hidden, norm_attn, wq, wkv, wo, cache, slot_entry, lengths, norm_mlp, w_gate, w_up, w_down):
    request_list = hidden.shape[0]
    queries_per_shared = QUERY_HEAD_COUNT // KEY_VALUE_HEADS
    normed_input = rms_scale(hidden, norm_attn)
    query_rows = jnp.dot(normed_input, wq, preferred_element_type=jnp.float32).reshape(request_list, QUERY_HEAD_COUNT, HEAD_SIZE)
    query_rows = narrow_rows(rotate(query_rows, lengths) * HEAD_SIZE ** (-0.5))
    fresh_keys = jnp.dot(normed_input, wkv[0], preferred_element_type=jnp.float32).reshape(request_list, KEY_VALUE_HEADS, HEAD_SIZE)
    fresh_keys = narrow_rows(rotate(fresh_keys, lengths))
    fresh_values = narrow_rows(jnp.dot(normed_input, wkv[1], preferred_element_type=jnp.float32)).reshape(request_list, KEY_VALUE_HEADS, HEAD_SIZE)
    grouped_queries = query_rows.reshape(request_list, KEY_VALUE_HEADS, queries_per_shared, HEAD_SIZE)

    def one_holder(holder):
        return holder_terms(holder, grouped_queries, cache, slot_entry, lengths)
    holder_max, holder_total, holder_output = lax.map(one_holder, jnp.arange(N_POOL, dtype=jnp.int32))
    pooled_slots = N_POOL * HOLDER_SLOTS
    holder_max = holder_max.reshape(pooled_slots, KEY_VALUE_HEADS, queries_per_shared)
    holder_total = holder_total.reshape(pooled_slots, KEY_VALUE_HEADS, queries_per_shared)
    holder_output = holder_output.reshape(pooled_slots, KEY_VALUE_HEADS, queries_per_shared, HEAD_SIZE)
    live_slot = slot_entry >= 0
    owners = jnp.where(live_slot, slot_entry // MAXB, 0)
    member = (jnp.arange(request_list, dtype=jnp.int32)[:, None] == owners[None, :]) & live_slot[None, :]
    cache_peak = lax.optimization_barrier(jnp.max(jnp.where(member[:, :, None, None], holder_max[None], NEGATIVE), axis=1))
    new_score = lax.optimization_barrier(jnp.sum(grouped_queries.astype(jnp.float32) * fresh_keys.astype(jnp.float32)[:, :, None, :], axis=-1))
    highest = jnp.maximum(cache_peak, new_score)
    rescale = jnp.exp(holder_max - highest[owners])
    new_weight = jnp.exp(new_score - highest)
    weight_sum = jax.ops.segment_sum(holder_total * rescale, owners, num_segments=request_list) + new_weight
    combined = jax.ops.segment_sum(holder_output * rescale[..., None], owners, num_segments=request_list)
    combined = combined + new_weight[..., None] * fresh_values.astype(jnp.float32)[:, :, None, :]
    attended = narrow_rows(combined / weight_sum[..., None]).reshape(request_list, QUERY_HEAD_COUNT * HEAD_SIZE)
    residual = narrow_rows(hidden.astype(jnp.float32) + jnp.dot(attended, wo, preferred_element_type=jnp.float32))
    mlp_in = rms_scale(residual, norm_mlp)
    gate = jnp.dot(mlp_in, w_gate, preferred_element_type=jnp.float32)
    upward = jnp.dot(mlp_in, w_up, preferred_element_type=jnp.float32)
    activation = narrow_rows(jax.nn.silu(gate) * upward)
    mlp_out = narrow_rows(jnp.dot(activation, w_down, preferred_element_type=jnp.float32))
    return (residual.astype(jnp.float32) + mlp_out.astype(jnp.float32)).astype(jnp.bfloat16)
```

```python
import math

import jax
import jax.numpy as jnp
from jax import lax
from jax.sharding import PartitionSpec as P

QUERY_HEAD_COUNT = 16
KEY_VALUE_HEADS = 8
HEAD_SIZE = 128


NEGATIVE = -1e30
EPSILON = 1e-05
ROPE_BASE = 1000000.0


def narrow_rows(tensor):
    return lax.optimization_barrier(tensor.astype(jnp.bfloat16))


def rms_scale(inputs, gain_vec):
    widened = inputs.astype(jnp.float32)
    mean_square = jnp.mean(widened * widened, axis=-1, keepdims=True)
    return narrow_rows(widened * lax.rsqrt(mean_square + EPSILON) * gain_vec.astype(jnp.float32))


def rotate(vectors, positions):
    head_width = vectors.shape[-1]
    halfway = head_width // 2
    frequency = jnp.exp(
        jnp.arange(halfway, dtype=jnp.float32) * (-2.0 * math.log(ROPE_BASE) / head_width)
    )
    angles = positions.astype(jnp.float32)[:, None] * frequency[None, :]
    cosine = jnp.cos(angles)[:, None, :]
    sine_of = jnp.sin(angles)[:, None, :]
    leading = vectors[..., :halfway]
    trailing = vectors[..., halfway:]
    return jnp.concatenate(
        [leading * cosine - trailing * sine_of, trailing * cosine + leading * sine_of], axis=-1
    )


def per_device(
    hidden, norm_attn, wq, wkv, wo, cache, slot_entry, lengths, norm_mlp, w_gate, w_up, w_down
):
    home_rows = hidden.shape[0]
    shared_heads = wkv.shape[2] // HEAD_SIZE
    queries_per_shared = QUERY_HEAD_COUNT // KEY_VALUE_HEADS
    query_heads = shared_heads * queries_per_shared
    home_index = lax.axis_index("pool")
    max_blocks = slot_entry.shape[0] * lax.axis_size("pool") // 16
    positions = lax.dynamic_slice_in_dim(lengths, home_index * home_rows, home_rows)
    normed_input = rms_scale(hidden, norm_attn)
    query_rows = jnp.dot(normed_input, wq, preferred_element_type=jnp.float32).reshape(
        home_rows, query_heads, HEAD_SIZE
    )
    query_rows = narrow_rows(rotate(query_rows, positions) * HEAD_SIZE ** (-0.5))
    fresh_keys = jnp.dot(normed_input, wkv[0], preferred_element_type=jnp.float32).reshape(
        home_rows, shared_heads, HEAD_SIZE
    )
    fresh_keys = narrow_rows(rotate(fresh_keys, positions))
    fresh_values = narrow_rows(
        jnp.dot(normed_input, wkv[1], preferred_element_type=jnp.float32)
    ).reshape(home_rows, shared_heads, HEAD_SIZE)
    every_query = lax.all_gather(
        query_rows.reshape(home_rows, query_heads * HEAD_SIZE), "pool", axis=0, tiled=True
    )
    request_list = every_query.shape[0]
    every_query = every_query.reshape(request_list, shared_heads, queries_per_shared, HEAD_SIZE)
    slot_count = slot_entry.shape[0]
    block_len = cache.shape[2]
    live_slot = slot_entry >= 0
    owners = jnp.where(live_slot, slot_entry // max_blocks, 0)
    block_index = jnp.where(live_slot, slot_entry % max_blocks, 0)
    position = block_index[:, None] * block_len + jnp.arange(block_len, dtype=jnp.int32)[None, :]
    in_range = live_slot[:, None] & (position < lengths[owners][:, None])
    token_owner = jnp.where(in_range, owners[:, None], -1).reshape(1, slot_count * block_len)
    keys = cache[0].reshape(slot_count * block_len, HEAD_SIZE)
    values = cache[1].reshape(slot_count * block_len, HEAD_SIZE)
    stacked = every_query.reshape(request_list, query_heads, HEAD_SIZE).transpose(1, 0, 2)
    stacked = stacked.reshape(query_heads * request_list, HEAD_SIZE)
    scores = lax.dot_general(
        stacked, keys, (((1,), (1,)), ((), ())), preferred_element_type=jnp.float32
    )
    row_owner = jnp.tile(jnp.arange(request_list, dtype=jnp.int32), query_heads)[:, None]
    taken = row_owner == token_owner
    scores = jnp.where(taken, scores, NEGATIVE)
    row_max = jnp.max(scores, axis=-1, keepdims=True)
    raised = jnp.where(taken, jnp.exp(scores - row_max), 0.0)
    row_total = jnp.sum(raised, axis=-1, keepdims=True)
    row_out = jnp.dot(raised.astype(jnp.bfloat16), values, preferred_element_type=jnp.float32)
    packed = jnp.concatenate(
        [row_out, jnp.broadcast_to(row_max, (row_max.shape[0], 64)),
         jnp.broadcast_to(row_total, (row_max.shape[0], 64))], axis=1
    ).reshape(query_heads, request_list, 256).transpose(1, 0, 2).reshape(request_list, query_heads * 256)
    arrived = lax.all_to_all(packed, "pool", split_axis=0, concat_axis=0, tiled=True)
    arrived = arrived.reshape(request_list, query_heads, 256)
    every_max = arrived[:, :, 128]
    part_max = jnp.max(every_max, axis=0, keepdims=True)
    factor = jnp.exp(every_max - part_max)
    part_total = jnp.sum(factor * arrived[:, :, 192], axis=0, keepdims=True)
    part_out = jnp.sum(factor[:, :, None] * arrived[:, :, :128], axis=0).reshape(1, query_heads * HEAD_SIZE)
    own_query = query_rows.reshape(home_rows, shared_heads, queries_per_shared, HEAD_SIZE).astype(
        jnp.float32
    )
    new_score = jnp.sum(own_query * fresh_keys.astype(jnp.float32)[:, :, None, :], axis=-1).reshape(
        home_rows, query_heads
    )
    highest = jnp.maximum(part_max, new_score)
    old_scale = jnp.exp(part_max - highest)
    new_scale = jnp.exp(new_score - highest)
    weight_sum = part_total * old_scale + new_scale
    new_term = (
        new_scale.reshape(home_rows, shared_heads, queries_per_shared)[..., None]
        * fresh_values.astype(jnp.float32)[:, :, None, :]
    )
    combined = part_out.reshape(home_rows, query_heads, HEAD_SIZE) * old_scale[
        ..., None
    ] + new_term.reshape(home_rows, query_heads, HEAD_SIZE)
    attended = narrow_rows(combined / weight_sum[..., None]).reshape(
        home_rows, query_heads * HEAD_SIZE
    )
    projected = lax.psum(jnp.dot(attended, wo, preferred_element_type=jnp.float32), "kv")
    residual = narrow_rows(hidden.astype(jnp.float32) + projected)
    mlp_in = rms_scale(residual, norm_mlp)
    columns = lax.all_to_all(mlp_in, "pool", split_axis=1, concat_axis=0, tiled=True)
    hidden_width = w_gate.shape[1]
    gate_term = jnp.dot(columns, w_gate, preferred_element_type=jnp.float32)
    up_term = jnp.dot(columns, w_up, preferred_element_type=jnp.float32)
    sent = jnp.concatenate([gate_term, up_term], axis=1).astype(jnp.bfloat16)
    summed = jnp.sum(
        lax.all_to_all(sent, "pool", split_axis=0, concat_axis=0, tiled=True).astype(jnp.float32),
        axis=0,
        keepdims=True,
    )
    activation = narrow_rows(jax.nn.silu(summed[:, :hidden_width]) * summed[:, hidden_width:])
    projected_down = jnp.dot(
        lax.all_gather(activation, "pool", axis=0, tiled=True),
        w_down,
        preferred_element_type=jnp.float32,
    )
    mlp_out = narrow_rows(lax.psum(projected_down, "kv"))
    returned = lax.all_to_all(mlp_out, "pool", split_axis=0, concat_axis=1, tiled=True)
    return (residual.astype(jnp.float32) + returned.astype(jnp.float32)).astype(jnp.bfloat16)


def solution(mesh):
    return jax.shard_map(
        per_device,
        mesh=mesh,
        in_specs=(
            P("pool", None),
            P(),
            P(None, "kv"),
            P(None, None, "kv"),
            P("kv", None),
            P(None, "pool", None, "kv"),
            P("pool"),
            P(),
            P(),
            P("pool", "kv"),
            P("pool", "kv"),
            P("kv", "pool"),
        ),
        out_specs=P("pool", None),
        check_vma=False,
    )
```

```python
import functools
import math

import jax
import jax.numpy as jnp
from jax import lax
from jax.experimental import pallas as pl
from jax.experimental.pallas import tpu as pltpu
from jax.sharding import PartitionSpec as P

HEAD_SIZE = 128
LANES = 128
NEGATIVE = -1e30
EPSILON = 1e-05
ROPE_BASE = 1000000.0
MESH = pl.DeviceIdType.MESH
F32 = jnp.float32
BF16 = jnp.bfloat16


def rounded(x):
    return x.astype(BF16).astype(F32)


def rms(x, gain):
    mean_square = jnp.mean(x * x, axis=-1, keepdims=True)
    return (x * lax.rsqrt(mean_square + EPSILON) * gain).astype(BF16)


def layer_kernel(
    pool, kv,
    hidden, norm_attn, wq, wkv, wo, cache, owner, cosine, sine, norm_mlp, w_gate, w_up, w_down,
    out,
    wide, gate_pad, up_pad, down_pad,
    q_send, q_recv, part_send, part_recv, proj_send, proj_recv, in_send, in_recv,
    gu_send, gu_recv, act_send, act_recv, down_send, down_recv, fin_send, fin_recv,
    send_sem, recv_sem,
):
    me = lax.axis_index("pool")
    my_kv = lax.axis_index("kv")
    quarter = lax.rem(me, 4)

    barrier = pltpu.get_barrier_semaphore()

    def greet_pool(k, carry):
        pl.semaphore_signal(
            barrier, inc=1, device_id={"pool": lax.rem(me + k, pool)}, device_id_type=MESH
        )
        return carry

    def greet_kv(k, carry):
        pl.semaphore_signal(
            barrier, inc=1, device_id={"kv": lax.rem(my_kv + k, kv)}, device_id_type=MESH
        )
        return carry

    lax.fori_loop(1, pool, greet_pool, 0)
    lax.fori_loop(1, kv, greet_kv, 0)

    def scatter(phase, source_of, target, axis, count, mine):
        def body(k, carry):
            peer = lax.rem(mine + k, count)
            pltpu.make_async_remote_copy(
                src_ref=source_of(peer),
                dst_ref=target.at[mine],
                send_sem=send_sem.at[phase],
                recv_sem=recv_sem.at[phase],
                device_id={axis: peer},
                device_id_type=MESH,
            ).start()
            return carry

        lax.fori_loop(1, count, body, 0)

    def arrive(phase, target, count):
        view = target.at[pl.ds(0, count - 1)]
        pltpu.make_async_copy(view, view, recv_sem.at[phase]).wait()

    def sent(phase, target, count):
        view = target.at[pl.ds(0, count - 1)]
        pltpu.make_async_copy(view, view, send_sem.at[phase]).wait()

    normed = rms(hidden[...].astype(F32), norm_attn[...].astype(F32))
    cos_row = cosine[...]
    sin_row = sine[...]

    def rotated(v):
        return v * cos_row + pltpu.roll(v, HEAD_SIZE // 2, 1) * sin_row

    q = jnp.dot(normed, wq[...], preferred_element_type=F32)
    scale = HEAD_SIZE ** (-0.5)
    q0 = rounded(rotated(q[:, :128]) * scale)
    q1 = rounded(rotated(q[:, 128:]) * scale)
    new_key = rounded(rotated(jnp.dot(normed, wkv[0], preferred_element_type=F32)))
    new_value = rounded(jnp.dot(normed, wkv[1], preferred_element_type=F32))
    own_q = jnp.concatenate([q0, q1], axis=1)
    q_send[0] = own_q
    q_recv[me] = own_q

    pl.semaphore_wait(barrier, pool - 1 + kv - 1)
    scatter(0, lambda peer: q_send.at[0], q_recv, "pool", pool, me)

    for g in range(4):
        here = quarter == g
        gate_pad[pl.ds(32 * g, 32), :] = jnp.where(here, w_gate[...].astype(F32), 0.0).astype(BF16)
        up_pad[pl.ds(32 * g, 32), :] = jnp.where(here, w_up[...].astype(F32), 0.0).astype(BF16)
    place = (
        lax.broadcasted_iota(jnp.int32, (32, LANES), 1)
        == lax.broadcasted_iota(jnp.int32, (32, LANES), 0) + 32 * quarter
    )
    down_pad[...] = jnp.dot(
        w_down[...], jnp.where(place, 1.0, 0.0).astype(BF16), preferred_element_type=F32
    ).astype(BF16)

    arrive(0, q_recv, pool)
    every = q_recv[:, 0, :]
    rows = jnp.concatenate([every[:, :128], every[:, 128:]], axis=0).astype(BF16)
    tokens = cache.shape[1]
    scores = lax.dot_general(rows, cache[0], (((1,), (1,)), ((), ())), preferred_element_type=F32)
    row_owner = lax.rem(lax.broadcasted_iota(jnp.int32, (2 * pool, 1), 0), pool)
    taken = row_owner == owner[...]
    scores = jnp.where(taken, scores, NEGATIVE)
    row_max = jnp.max(scores, axis=1, keepdims=True)
    raised = jnp.where(taken, jnp.exp(scores - row_max), 0.0)
    row_total = jnp.sum(raised, axis=1, keepdims=True)
    row_out = jnp.dot(raised.astype(BF16), cache[1], preferred_element_type=F32)
    lane = lax.broadcasted_iota(jnp.int32, (pool, LANES), 1)
    stats = jnp.where(
        lane == 0,
        row_max[:pool],
        jnp.where(lane == 1, row_max[pool:], jnp.where(lane == 2, row_total[:pool], row_total[pool:])),
    )
    wide[:, 0:128] = row_out[:pool]
    wide[:, 128:256] = row_out[pool:]
    wide[:, 256:384] = stats

    def spread(target, width):
        def body(b, carry):
            block = wide[pl.ds(pl.multiple_of(b * 8, 8), 8), 0:width]
            for i in range(8):
                target[b * 8 + i] = block[i : i + 1]
            return carry

        lax.fori_loop(0, pool // 8, body, 0)

    spread(part_send, 384)
    part_recv[me] = part_send[me]
    scatter(1, lambda peer: part_send.at[peer], part_recv, "pool", pool, me)

    arrive(1, part_recv, pool)
    parts = part_recv[:, 0, :]
    heads = []
    for j, qj in ((0, q0), (1, q1)):
        maxima = parts[:, 256 + j : 257 + j]
        totals = parts[:, 258 + j : 259 + j]
        new_score = jnp.sum(qj * new_key, axis=1, keepdims=True)
        highest = jnp.maximum(jnp.max(maxima, axis=0, keepdims=True), new_score)
        factor = jnp.exp(maxima - highest)
        new_factor = jnp.exp(new_score - highest)
        weight = jnp.sum(totals * factor, axis=0, keepdims=True) + new_factor
        mixed = jnp.sum(parts[:, 128 * j : 128 * (j + 1)] * factor, axis=0, keepdims=True)
        heads.append((mixed + new_factor * new_value) / weight)
    attended = jnp.concatenate(heads, axis=1).astype(BF16)
    projected = jnp.dot(attended, wo[...], preferred_element_type=F32)
    proj_send[0] = projected
    proj_recv[my_kv] = projected
    scatter(2, lambda peer: proj_send.at[0], proj_recv, "kv", kv, my_kv)
    arrive(2, proj_recv, kv)
    total = proj_recv[0]
    for k in range(1, kv):
        total = total + proj_recv[k]
    residual = rounded(hidden[...].astype(F32) + total)
    mlp_in = rms(residual, norm_mlp[...].astype(F32)).astype(F32)
    groups = mlp_in.shape[1] // LANES
    for g in range(groups):
        in_send[g] = mlp_in[:, g * LANES : (g + 1) * LANES]
    in_recv[me] = in_send[me // 4]
    scatter(3, lambda peer: in_send.at[peer // 4], in_recv, "pool", pool, me)

    arrive(3, in_recv, pool)
    columns = in_recv[:, 0, :].astype(BF16)
    half = w_gate.shape[1]
    wide[:, 0:half] = jnp.dot(columns, gate_pad[...], preferred_element_type=F32)
    wide[:, half : 2 * half] = jnp.dot(columns, up_pad[...], preferred_element_type=F32)

    def spread_gu(b, carry):
        at = pl.ds(pl.multiple_of(b * 8, 8), 8)
        gate_rows = wide[at, 0:half]
        up_rows = wide[at, half : 2 * half]
        for i in range(8):
            both = jnp.concatenate([gate_rows[i : i + 1], up_rows[i : i + 1]], axis=0)
            gu_send[b * 8 + i] = both.astype(BF16)
        return carry

    lax.fori_loop(0, pool // 8, spread_gu, 0)
    gu_recv[me] = gu_send[me]
    scatter(4, lambda peer: gu_send.at[peer], gu_recv, "pool", pool, me)
    arrive(4, gu_recv, pool)
    summed = jnp.sum(gu_recv[...].astype(F32), axis=0)
    gate = summed[0:1]
    up = summed[1:2]
    activation = gate / (1.0 + jnp.exp(-gate)) * up
    act_row = rounded(activation)
    act_send[0] = act_row
    act_recv[me] = act_row
    scatter(5, lambda peer: act_send.at[0], act_recv, "pool", pool, me)

    arrive(5, act_recv, pool)
    activations = act_recv[:, 0, :].astype(BF16)
    wide[:, 0:LANES] = jnp.dot(activations, down_pad[...], preferred_element_type=F32)

    spread(down_send, LANES)
    down_recv[me] = down_send[me]
    scatter(6, lambda peer: down_send.at[peer], down_recv, "pool", pool, me)
    arrive(6, down_recv, pool)
    pieces = []
    for g in range(groups):
        piece = down_recv[4 * g]
        for j in range(1, 4):
            piece = piece + down_recv[4 * g + j]
        pieces.append(piece)
    down_row = jnp.concatenate(pieces, axis=1)
    fin_send[0] = down_row
    fin_recv[my_kv] = down_row
    scatter(7, lambda peer: fin_send.at[0], fin_recv, "kv", kv, my_kv)
    arrive(7, fin_recv, kv)
    total = fin_recv[0]
    for k in range(1, kv):
        total = total + fin_recv[k]
    out[...] = (residual + rounded(total)).astype(BF16)

    sent(0, q_recv, pool)
    sent(1, part_recv, pool)
    sent(2, proj_recv, kv)
    sent(3, in_recv, pool)
    sent(4, gu_recv, pool)
    sent(5, act_recv, pool)
    sent(6, down_recv, pool)
    sent(7, fin_recv, kv)


def per_device(
    hidden, norm_attn, wq, wkv, wo, cache, slot_entry, lengths, norm_mlp, w_gate, w_up, w_down,
    pool, kv,
):
    width = hidden.shape[1]
    half = w_gate.shape[1]
    home = lax.axis_index("pool")
    slot_count = slot_entry.shape[0]
    block_len = cache.shape[2]
    requests = lengths.shape[0]
    max_blocks = 64
    position = lax.dynamic_slice_in_dim(lengths, home, 1).astype(F32)
    halfway = HEAD_SIZE // 2
    frequency = jnp.exp(
        jnp.arange(halfway, dtype=F32) * (-2.0 * math.log(ROPE_BASE) / HEAD_SIZE)
    )
    angles = position[:, None] * frequency[None, :]
    cosine = jnp.cos(angles)
    sine = jnp.sin(angles)
    cosine = jnp.concatenate([cosine, cosine], axis=1)
    sine = jnp.concatenate([-sine, sine], axis=1)
    live = slot_entry >= 0
    owners = jnp.where(live, slot_entry // max_blocks, -1)
    blocks = jnp.where(live, slot_entry % max_blocks, 0)
    hit = owners[:, None] == jnp.arange(requests, dtype=jnp.int32)[None, :]
    extent = jnp.sum(jnp.where(hit, lengths[None, :], 0), axis=1)
    places = blocks[:, None] * block_len + jnp.arange(block_len, dtype=jnp.int32)[None, :]
    owner = jnp.where(places < extent[:, None], owners[:, None], -1)
    owner = owner.reshape(1, slot_count * block_len)
    vmem = pl.BlockSpec(memory_space=pltpu.VMEM)
    return pl.pallas_call(
        functools.partial(layer_kernel, pool, kv),
        out_shape=jax.ShapeDtypeStruct((1, width), BF16),
        in_specs=[vmem] * 13,
        out_specs=vmem,
        scratch_shapes=[
            pltpu.VMEM((pool, 2 * half), F32),
            pltpu.VMEM((LANES, half), BF16),
            pltpu.VMEM((LANES, half), BF16),
            pltpu.VMEM((half, LANES), BF16),
            pltpu.VMEM((1, 1, 256), F32),
            pltpu.VMEM((pool, 1, 256), F32),
            pltpu.VMEM((pool, 1, 384), F32),
            pltpu.VMEM((pool, 1, 384), F32),
            pltpu.VMEM((1, 1, width), F32),
            pltpu.VMEM((kv, 1, width), F32),
            pltpu.VMEM((width // LANES, 1, LANES), F32),
            pltpu.VMEM((pool, 1, LANES), F32),
            pltpu.VMEM((pool, 2, half), BF16),
            pltpu.VMEM((pool, 2, half), BF16),
            pltpu.VMEM((1, 1, half), F32),
            pltpu.VMEM((pool, 1, half), F32),
            pltpu.VMEM((pool, 1, LANES), F32),
            pltpu.VMEM((pool, 1, LANES), F32),
            pltpu.VMEM((1, 1, width), F32),
            pltpu.VMEM((kv, 1, width), F32),
            pltpu.SemaphoreType.DMA((8,)),
            pltpu.SemaphoreType.DMA((8,)),
        ],
        compiler_params=pltpu.CompilerParams(
            collective_id=0, has_side_effects=True, vmem_limit_bytes=48 * 1024 * 1024
        ),
    )(
        hidden, norm_attn.reshape(1, width), wq, wkv, wo,
        cache.reshape(2, slot_count * block_len, HEAD_SIZE), owner, cosine, sine,
        norm_mlp.reshape(1, width), w_gate, w_up, w_down,
    )


def solution(mesh):
    return jax.shard_map(
        functools.partial(per_device, pool=mesh.shape["pool"], kv=mesh.shape["kv"]),
        mesh=mesh,
        in_specs=(
            P("pool", None),
            P(),
            P(None, "kv"),
            P(None, None, "kv"),
            P("kv", None),
            P(None, "pool", None, "kv"),
            P("pool"),
            P(),
            P(),
            P("pool", "kv"),
            P("pool", "kv"),
            P("kv", "pool"),
        ),
        out_specs=P("pool", None),
        check_vma=False,
    )
```

```python
import functools
import math

import jax
import jax.numpy as jnp
from jax import lax
from jax.experimental import pallas as pl
from jax.experimental.pallas import tpu as pltpu
from jax.sharding import PartitionSpec as P

HEAD_SIZE = 128
LANES = 128
NEGATIVE = -1e30
EPSILON = 1e-05
ROPE_BASE = 1000000.0
MESH = pl.DeviceIdType.MESH
F32 = jnp.float32
BF16 = jnp.bfloat16


def rounded(x):
    return x.astype(BF16).astype(F32)


def rms(x, gain):
    mean_square = jnp.mean(x * x, axis=-1, keepdims=True)
    return (x * lax.rsqrt(mean_square + EPSILON) * gain).astype(BF16)


def turned(angles):
    turns = jnp.floor(angles * (2.0 / math.pi) + 0.5)
    rest = ((angles - turns * 1.5703125) - turns * 4.837512969970703125e-4) - turns * 7.54978995489188216e-8
    square = rest * rest
    sine = rest + rest * square * (
        -1.6666654611e-1 + square * (8.3321608736e-3 - 1.9515295891e-4 * square)
    )
    cosine = 1.0 - 0.5 * square + square * square * (
        4.166664568298827e-2 + square * (-1.388731625493765e-3 + 2.443315711809948e-5 * square)
    )
    quadrant = turns - 4.0 * jnp.floor(turns * 0.25)
    odd = (quadrant == 1.0) | (quadrant == 3.0)
    cos_sign = jnp.where((quadrant == 1.0) | (quadrant == 2.0), -1.0, 1.0)
    sin_sign = jnp.where(quadrant >= 2.0, -1.0, 1.0)
    return jnp.where(odd, sine, cosine) * cos_sign, jnp.where(odd, cosine, sine) * sin_sign


def flat(tile):
    return jnp.concatenate([tile[i : i + 1] for i in range(tile.shape[0])], axis=1)


def layer_kernel(
    pool, kv,
    slot_entry, lengths, hidden_hbm, norm_attn_hbm, wq_hbm, wkv_hbm, wo_hbm, cache_hbm,
    norm_mlp_hbm, w_gate, w_up, w_down,
    out,
    hidden, norm_attn, norm_mlp, wq, wkv, wo, cache,
    wide, gate_pad, up_pad, down_pad,
    q_send, q_recv, part_send, part_recv, proj_send, proj_recv, in_send, in_recv,
    gu_send, gu_recv, act_send, act_recv, down_send, down_recv, fin_send, fin_recv,
    send_sem, recv_sem, load_sem,
):
    me = lax.axis_index("pool")
    my_kv = lax.axis_index("kv")
    quarter = lax.rem(me, 4)

    barrier = pltpu.get_barrier_semaphore()

    def greet_pool(k, carry):
        pl.semaphore_signal(
            barrier, inc=1, device_id={"pool": lax.rem(me + k, pool)}, device_id_type=MESH
        )
        return carry

    def greet_kv(k, carry):
        pl.semaphore_signal(
            barrier, inc=1, device_id={"kv": lax.rem(my_kv + k, kv)}, device_id_type=MESH
        )
        return carry

    loads = [
        pltpu.make_async_copy(source, target, load_sem.at[i])
        for i, (source, target) in enumerate(
            [(hidden_hbm, hidden), (norm_attn_hbm, norm_attn), (wq_hbm, wq), (wkv_hbm, wkv),
             (cache_hbm, cache), (wo_hbm, wo), (norm_mlp_hbm, norm_mlp)]
            + [
                (source, target.at[pl.ds(32 * g, 32), :])
                for source, target in ((w_gate, gate_pad), (w_up, up_pad), (w_down, down_pad))
                for g in range(4)
            ]
        )
    ]
    for load in loads[:4]:
        load.start()
    lax.fori_loop(1, pool, greet_pool, 0, unroll=9)
    lax.fori_loop(1, kv, greet_kv, 0, unroll=7)
    for load in loads[4:]:
        load.start()

    my_y = me // 16
    my_z = lax.rem(me, 16)

    def scatter(phase, source_of, target, axis, mine):
        def send(peer):
            pltpu.make_async_remote_copy(
                src_ref=source_of(peer),
                dst_ref=target.at[mine],
                send_sem=send_sem.at[phase],
                recv_sem=recv_sem.at[phase],
                device_id={axis: peer},
                device_id_type=MESH,
            ).start()

        if axis == "kv":
            for k in range(1, kv):
                send(lax.rem(mine + k, kv))
            return

        def at(dy, z):
            send(lax.rem(my_y + dy, 4) * 16 + z)

        def body(t, carry):
            step = (t + 1) // 2
            z = lax.rem(my_z + 24 + (2 * lax.rem(t, 2) - 1) * step, 16)
            for dy in (2, 1, 3, 0):
                at(dy, z)
            return carry

        lax.fori_loop(0, 15, body, 0)
        for dy in (2, 1, 3):
            at(dy, my_z)

    def arrive(phase, target, count):
        view = target.at[pl.ds(0, count - 1)]
        pltpu.make_async_copy(view, view, recv_sem.at[phase]).wait()

    def sent(phase, target, count):
        view = target.at[pl.ds(0, count - 1)]
        pltpu.make_async_copy(view, view, send_sem.at[phase]).wait()

    half_lane = lax.rem(lax.broadcasted_iota(jnp.int32, (1, LANES), 1), HEAD_SIZE // 2)
    frequency = jnp.exp(half_lane.astype(F32) * (-2.0 * math.log(ROPE_BASE) / HEAD_SIZE))
    position = jnp.full((1, LANES), lengths[me], jnp.int32).astype(F32)
    cos_row, sin_row = turned(position * frequency)
    lanes = lax.broadcasted_iota(jnp.int32, (1, LANES), 1)
    sin_row = jnp.where(lanes < HEAD_SIZE // 2, -sin_row, sin_row)
    owned = []
    for i in range(slot_entry.shape[0]):
        entry = slot_entry[i]
        holder_of = jnp.maximum(entry, 0) // 64
        left = lengths[holder_of] - (jnp.maximum(entry, 0) - holder_of * 64) * LANES
        left = jnp.where(entry >= 0, left, 0)
        owned.append(jnp.where(lanes < left, holder_of, -1))
    owner = jnp.concatenate(owned, axis=1)
    loads[0].wait()
    loads[1].wait()
    normed = rms(hidden[...].astype(F32), flat(norm_attn[...].astype(F32)))
    loads[2].wait()
    loads[3].wait()

    def rotated(v):
        return v * cos_row + pltpu.roll(v, HEAD_SIZE // 2, 1) * sin_row

    q = jnp.dot(normed, wq[...], preferred_element_type=F32)
    scale = HEAD_SIZE ** (-0.5)
    q0 = rounded(rotated(q[:, :128]) * scale)
    q1 = rounded(rotated(q[:, 128:]) * scale)
    new_key = rounded(rotated(jnp.dot(normed, wkv[0], preferred_element_type=F32)))
    new_value = rounded(jnp.dot(normed, wkv[1], preferred_element_type=F32))
    own_q = jnp.concatenate([q0, q1], axis=1)
    q_send[0] = own_q
    q_recv[me] = own_q

    pl.semaphore_wait(barrier, pool - 1 + kv - 1)
    scatter(0, lambda peer: q_send.at[0], q_recv, "pool", me)

    for load in loads[4:]:
        load.wait()
    own_lanes = lax.broadcasted_iota(jnp.int32, (pool, LANES), 1) // 32 == quarter
    mlp_gain = flat(norm_mlp[...].astype(F32))

    arrive(0, q_recv, pool)
    every = q_recv[:, 0, :]
    rows = jnp.concatenate([every[:, :128], every[:, 128:]], axis=0).astype(BF16)
    scores = lax.dot_general(rows, cache[0], (((1,), (1,)), ((), ())), preferred_element_type=F32)
    row_owner = lax.rem(lax.broadcasted_iota(jnp.int32, (2 * pool, 1), 0), pool)
    taken = row_owner == owner
    scores = jnp.where(taken, scores, NEGATIVE)
    row_max = jnp.max(scores, axis=1, keepdims=True)
    raised = jnp.where(taken, jnp.exp(scores - row_max), 0.0)
    row_total = jnp.sum(raised, axis=1, keepdims=True)
    row_out = jnp.dot(raised.astype(BF16), cache[1], preferred_element_type=F32)
    lane = lax.broadcasted_iota(jnp.int32, (pool, LANES), 1)
    stats = jnp.where(
        lane == 0,
        row_max[:pool],
        jnp.where(lane == 1, row_max[pool:], jnp.where(lane == 2, row_total[:pool], row_total[pool:])),
    )
    wide[:, 0:128] = row_out[:pool]
    wide[:, 128:256] = row_out[pool:]
    wide[:, 256:384] = stats

    def spread(target, width):
        def body(b, carry):
            block = wide[pl.ds(pl.multiple_of(b * 8, 8), 8), 0:width]
            for i in range(8):
                target[b * 8 + i] = block[i : i + 1]
            return carry

        lax.fori_loop(0, pool // 8, body, 0)

    spread(part_send, 384)
    part_recv[me] = part_send[me]
    scatter(1, lambda peer: part_send.at[peer], part_recv, "pool", me)

    arrive(1, part_recv, pool)
    parts = part_recv[:, 0, :]
    heads = []
    for j, qj in ((0, q0), (1, q1)):
        maxima = parts[:, 256 + j : 257 + j]
        totals = parts[:, 258 + j : 259 + j]
        new_score = jnp.sum(qj * new_key, axis=1, keepdims=True)
        highest = jnp.maximum(jnp.max(maxima, axis=0, keepdims=True), new_score)
        factor = jnp.exp(maxima - highest)
        new_factor = jnp.exp(new_score - highest)
        weight = jnp.sum(totals * factor, axis=0, keepdims=True) + new_factor
        mixed = jnp.sum(parts[:, 128 * j : 128 * (j + 1)] * factor, axis=0, keepdims=True)
        heads.append((mixed + new_factor * new_value) / weight)
    attended = jnp.concatenate(heads, axis=1).astype(BF16)
    projected = jnp.dot(attended, wo[...], preferred_element_type=F32)
    proj_send[0] = projected
    proj_recv[my_kv] = projected
    scatter(2, lambda peer: proj_send.at[0], proj_recv, "kv", my_kv)
    arrive(2, proj_recv, kv)
    total = proj_recv[0]
    for k in range(1, kv):
        total = total + proj_recv[k]
    residual = rounded(hidden[...].astype(F32) + total)
    mlp_in = rms(residual, mlp_gain).astype(F32)
    groups = mlp_in.shape[1] // LANES
    for g in range(groups):
        in_send[g] = mlp_in[:, g * LANES : (g + 1) * LANES]
    in_recv[me] = in_send[me // 4]
    scatter(3, lambda peer: in_send.at[peer // 4], in_recv, "pool", me)

    arrive(3, in_recv, pool)
    columns = jnp.where(own_lanes, in_recv[:, 0, :], 0.0).astype(BF16)
    half = w_gate.shape[1]
    wide[:, 0:half] = jnp.dot(columns, gate_pad[...], preferred_element_type=F32)
    wide[:, half : 2 * half] = jnp.dot(columns, up_pad[...], preferred_element_type=F32)

    def spread_gu(b, carry):
        at = pl.ds(pl.multiple_of(b * 8, 8), 8)
        gate_rows = wide[at, 0:half]
        up_rows = wide[at, half : 2 * half]
        for i in range(8):
            both = jnp.concatenate([gate_rows[i : i + 1], up_rows[i : i + 1]], axis=0)
            gu_send[b * 8 + i] = both.astype(BF16)
        return carry

    lax.fori_loop(0, pool // 8, spread_gu, 0)
    gu_recv[me] = gu_send[me]
    scatter(4, lambda peer: gu_send.at[peer], gu_recv, "pool", me)
    arrive(4, gu_recv, pool)
    summed = jnp.sum(gu_recv[...].astype(F32), axis=0)
    gate = summed[0:1]
    up = summed[1:2]
    activation = gate / (1.0 + jnp.exp(-gate)) * up
    middle = half // 2
    act_row = jnp.concatenate([activation[:, :middle], activation[:, middle:]], axis=0).astype(BF16)
    act_send[0] = act_row
    act_recv[me] = act_row
    scatter(5, lambda peer: act_send.at[0], act_recv, "pool", me)

    arrive(5, act_recv, pool)
    activations = act_recv[...].astype(F32)
    activations = jnp.concatenate([activations[:, 0, :], activations[:, 1, :]], axis=1).astype(BF16)
    down = lax.dot_general(
        activations, down_pad[...], (((1,), (1,)), ((), ())), preferred_element_type=F32
    )
    wide[:, 0:LANES] = jnp.where(own_lanes, down, 0.0)

    spread(down_send, LANES)
    down_recv[me] = down_send[me]
    scatter(6, lambda peer: down_send.at[peer], down_recv, "pool", me)
    arrive(6, down_recv, pool)
    pieces = []
    for g in range(groups):
        piece = down_recv[4 * g]
        for j in range(1, 4):
            piece = piece + down_recv[4 * g + j]
        pieces.append(piece)
    down_row = jnp.concatenate(pieces, axis=1)
    fin_send[0] = down_row
    fin_recv[my_kv] = down_row
    scatter(7, lambda peer: fin_send.at[0], fin_recv, "kv", my_kv)
    arrive(7, fin_recv, kv)
    total = fin_recv[0]
    for k in range(1, kv):
        total = total + fin_recv[k]
    out[...] = (residual + rounded(total)).astype(BF16)

    sent(0, q_recv, pool)
    sent(1, part_recv, pool)
    sent(2, proj_recv, kv)
    sent(3, in_recv, pool)
    sent(4, gu_recv, pool)
    sent(5, act_recv, pool)
    sent(6, down_recv, pool)
    sent(7, fin_recv, kv)


def per_device(
    hidden, norm_attn, wq, wkv, wo, cache, slot_entry, lengths, norm_mlp, w_gate, w_up, w_down,
    pool, kv,
):
    width = hidden.shape[1]
    half = w_gate.shape[1]
    tokens = cache.shape[1] * cache.shape[2]
    smem = pl.BlockSpec(memory_space=pltpu.SMEM)
    hbm = pl.BlockSpec(memory_space=pltpu.HBM)
    vmem = pl.BlockSpec(memory_space=pltpu.VMEM)
    return pl.pallas_call(
        functools.partial(layer_kernel, pool, kv),
        out_shape=jax.ShapeDtypeStruct((1, width), BF16),
        in_specs=[smem] * 2 + [hbm] * 10,
        out_specs=vmem,
        scratch_shapes=[
            pltpu.VMEM((1, width), BF16),
            pltpu.VMEM((width // LANES, LANES), BF16),
            pltpu.VMEM((width // LANES, LANES), BF16),
            pltpu.VMEM(wq.shape, BF16),
            pltpu.VMEM(wkv.shape, BF16),
            pltpu.VMEM(wo.shape, BF16),
            pltpu.VMEM((2, tokens, HEAD_SIZE), BF16),
            pltpu.VMEM((pool, 2 * half), F32),
            pltpu.VMEM((LANES, half), BF16),
            pltpu.VMEM((LANES, half), BF16),
            pltpu.VMEM((LANES, half), BF16),
            pltpu.VMEM((1, 1, 256), F32),
            pltpu.VMEM((pool, 1, 256), F32),
            pltpu.VMEM((pool, 1, 384), F32),
            pltpu.VMEM((pool, 1, 384), F32),
            pltpu.VMEM((1, 1, width), F32),
            pltpu.VMEM((kv, 1, width), F32),
            pltpu.VMEM((width // LANES, 1, LANES), F32),
            pltpu.VMEM((pool, 1, LANES), F32),
            pltpu.VMEM((pool, 2, half), BF16),
            pltpu.VMEM((pool, 2, half), BF16),
            pltpu.VMEM((1, 2, half // 2), BF16),
            pltpu.VMEM((pool, 2, half // 2), BF16),
            pltpu.VMEM((pool, 1, LANES), F32),
            pltpu.VMEM((pool, 1, LANES), F32),
            pltpu.VMEM((1, 1, width), F32),
            pltpu.VMEM((kv, 1, width), F32),
            pltpu.SemaphoreType.DMA((8,)),
            pltpu.SemaphoreType.DMA((8,)),
            pltpu.SemaphoreType.DMA((19,)),
        ],
        compiler_params=pltpu.CompilerParams(
            collective_id=0, has_side_effects=True, vmem_limit_bytes=67043328
        ),
    )(
        slot_entry, lengths, hidden, norm_attn.reshape(width // LANES, LANES), wq, wkv, wo,
        cache.reshape(2, tokens, HEAD_SIZE), norm_mlp.reshape(width // LANES, LANES),
        w_gate, w_up, w_down.T,
    )


def solution(mesh):
    return jax.shard_map(
        functools.partial(per_device, pool=mesh.shape["pool"], kv=mesh.shape["kv"]),
        mesh=mesh,
        in_specs=(
            P("pool", None),
            P(),
            P(None, "kv"),
            P(None, None, "kv"),
            P("kv", None),
            P(None, "pool", None, "kv"),
            P("pool"),
            P(),
            P(),
            P("pool", "kv"),
            P("pool", "kv"),
            P("kv", "pool"),
        ),
        out_specs=P("pool", None),
        check_vma=False,
    )
```

```python
import functools
import math

import jax
import jax.numpy as jnp
from jax import lax
from jax.experimental import pallas as pl
from jax.experimental.pallas import tpu as pltpu
from jax.sharding import PartitionSpec as P

HEAD_SIZE = 128
LANES = 128
NEGATIVE = -1e30
EPSILON = 1e-05
ROPE_BASE = 1000000.0
MESH = pl.DeviceIdType.MESH
F32 = jnp.float32
BF16 = jnp.bfloat16


def rounded(x):
    return x.astype(BF16).astype(F32)


def rms(x, gain):
    mean_square = jnp.mean(x * x, axis=-1, keepdims=True)
    return (x * lax.rsqrt(mean_square + EPSILON) * gain).astype(BF16)


def turned(angles):
    turns = jnp.floor(angles * (2.0 / math.pi) + 0.5)
    rest = ((angles - turns * 1.5703125) - turns * 4.837512969970703125e-4) - turns * 7.54978995489188216e-8
    square = rest * rest
    sine = rest + rest * square * (
        -1.6666654611e-1 + square * (8.3321608736e-3 - 1.9515295891e-4 * square)
    )
    cosine = 1.0 - 0.5 * square + square * square * (
        4.166664568298827e-2 + square * (-1.388731625493765e-3 + 2.443315711809948e-5 * square)
    )
    quadrant = turns - 4.0 * jnp.floor(turns * 0.25)
    odd = (quadrant == 1.0) | (quadrant == 3.0)
    cos_sign = jnp.where((quadrant == 1.0) | (quadrant == 2.0), -1.0, 1.0)
    sin_sign = jnp.where(quadrant >= 2.0, -1.0, 1.0)
    return jnp.where(odd, sine, cosine) * cos_sign, jnp.where(odd, cosine, sine) * sin_sign


def flat(tile):
    return jnp.concatenate([tile[i : i + 1] for i in range(tile.shape[0])], axis=1)


def layer_kernel(
    pool, kv,
    slot_entry, lengths, hidden_hbm, norm_attn_hbm, wq_hbm, wkv_hbm, wo_hbm, cache_hbm,
    norm_mlp_hbm, w_gate, w_up, w_down,
    out,
    hidden, norm_attn, norm_mlp, wq, wkv, wo, cache,
    wide, gate_pad, up_pad, down_pad,
    q_send, q_recv, part_send, part_recv, proj_send, proj_recv, in_send, in_recv,
    gu_send, gu_mid, gu_half, gu_recv, act_send, act_recv, down_send, down_recv, fin_send, fin_recv,
    send_sem, recv_sem, load_sem,
):
    me = lax.axis_index("pool")
    my_kv = lax.axis_index("kv")
    quarter = lax.rem(me, 4)

    barrier = pltpu.get_barrier_semaphore()

    def greet_pool(k, carry):
        pl.semaphore_signal(
            barrier, inc=1, device_id={"pool": lax.rem(me + k, pool)}, device_id_type=MESH
        )
        return carry

    def greet_kv(k, carry):
        pl.semaphore_signal(
            barrier, inc=1, device_id={"kv": lax.rem(my_kv + k, kv)}, device_id_type=MESH
        )
        return carry

    loads = [
        pltpu.make_async_copy(source, target, load_sem.at[i])
        for i, (source, target) in enumerate(
            [(hidden_hbm, hidden), (norm_attn_hbm, norm_attn), (wq_hbm, wq), (wkv_hbm, wkv),
             (cache_hbm, cache), (wo_hbm, wo), (norm_mlp_hbm, norm_mlp)]
            + [
                (source, target.at[pl.ds(32 * g, 32), :])
                for source, target in ((w_gate, gate_pad), (w_up, up_pad), (w_down, down_pad))
                for g in range(4)
            ]
        )
    ]
    for load in loads[:4]:
        load.start()
    lax.fori_loop(1, pool, greet_pool, 0, unroll=9)
    lax.fori_loop(1, kv, greet_kv, 0, unroll=7)
    for load in loads[4:]:
        load.start()

    my_y = me // 16
    my_z = lax.rem(me, 16)

    def scatter(phase, source_of, target, axis, mine):
        def send(peer):
            pltpu.make_async_remote_copy(
                src_ref=source_of(peer),
                dst_ref=target.at[mine],
                send_sem=send_sem.at[phase],
                recv_sem=recv_sem.at[phase],
                device_id={axis: peer},
                device_id_type=MESH,
            ).start()

        if axis == "kv":
            for k in range(1, kv):
                send(lax.rem(mine + k, kv))
            return

        def at(dy, z):
            send(lax.rem(my_y + dy, 4) * 16 + z)

        def body(t, carry):
            step = (t + 1) // 2
            z = lax.rem(my_z + 24 + (2 * lax.rem(t, 2) - 1) * step, 16)
            for dy in (2, 1, 3, 0):
                at(dy, z)
            return carry

        lax.fori_loop(0, 15, body, 0)
        for dy in (2, 1, 3):
            at(dy, my_z)

    def arrive(phase, target, count):
        view = target.at[pl.ds(0, count - 1)]
        pltpu.make_async_copy(view, view, recv_sem.at[phase]).wait()

    def sent(phase, target, count):
        view = target.at[pl.ds(0, count - 1)]
        pltpu.make_async_copy(view, view, send_sem.at[phase]).wait()

    half_lane = lax.rem(lax.broadcasted_iota(jnp.int32, (1, LANES), 1), HEAD_SIZE // 2)
    frequency = jnp.exp(half_lane.astype(F32) * (-2.0 * math.log(ROPE_BASE) / HEAD_SIZE))
    position = jnp.full((1, LANES), lengths[me], jnp.int32).astype(F32)
    cos_row, sin_row = turned(position * frequency)
    lanes = lax.broadcasted_iota(jnp.int32, (1, LANES), 1)
    sin_row = jnp.where(lanes < HEAD_SIZE // 2, -sin_row, sin_row)
    owned = []
    for i in range(slot_entry.shape[0]):
        entry = slot_entry[i]
        holder_of = jnp.maximum(entry, 0) // 64
        left = lengths[holder_of] - (jnp.maximum(entry, 0) - holder_of * 64) * LANES
        left = jnp.where(entry >= 0, left, 0)
        owned.append(jnp.where(lanes < left, holder_of, -1))
    owner = jnp.concatenate(owned, axis=1)
    loads[0].wait()
    loads[1].wait()
    normed = rms(hidden[...].astype(F32), flat(norm_attn[...].astype(F32)))
    loads[2].wait()
    loads[3].wait()

    def rotated(v):
        return v * cos_row + pltpu.roll(v, HEAD_SIZE // 2, 1) * sin_row

    q = jnp.dot(normed, wq[...], preferred_element_type=F32)
    scale = HEAD_SIZE ** (-0.5)
    q0 = rounded(rotated(q[:, :128]) * scale)
    q1 = rounded(rotated(q[:, 128:]) * scale)
    new_key = rounded(rotated(jnp.dot(normed, wkv[0], preferred_element_type=F32)))
    new_value = rounded(jnp.dot(normed, wkv[1], preferred_element_type=F32))
    own_q = jnp.concatenate([q0, q1], axis=1)
    q_send[0] = own_q
    q_recv[me] = own_q

    pl.semaphore_wait(barrier, pool - 1 + kv - 1)
    scatter(0, lambda peer: q_send.at[0], q_recv, "pool", me)

    for load in loads[4:]:
        load.wait()
    own_lanes = lax.broadcasted_iota(jnp.int32, (pool, LANES), 1) // 32 == quarter
    mlp_gain = flat(norm_mlp[...].astype(F32))

    arrive(0, q_recv, pool)
    every = q_recv[:, 0, :]
    rows = jnp.concatenate([every[:, :128], every[:, 128:]], axis=0).astype(BF16)
    scores = lax.dot_general(rows, cache[0], (((1,), (1,)), ((), ())), preferred_element_type=F32)
    row_owner = lax.rem(lax.broadcasted_iota(jnp.int32, (2 * pool, 1), 0), pool)
    taken = row_owner == owner
    scores = jnp.where(taken, scores, NEGATIVE)
    row_max = jnp.max(scores, axis=1, keepdims=True)
    raised = jnp.where(taken, jnp.exp(scores - row_max), 0.0)
    row_total = jnp.sum(raised, axis=1, keepdims=True)
    row_out = jnp.dot(raised.astype(BF16), cache[1], preferred_element_type=F32)
    lane = lax.broadcasted_iota(jnp.int32, (pool, LANES), 1)
    stats = jnp.where(
        lane == 0,
        row_max[:pool],
        jnp.where(lane == 1, row_max[pool:], jnp.where(lane == 2, row_total[:pool], row_total[pool:])),
    )
    wide[:, 0:128] = row_out[:pool]
    wide[:, 128:256] = row_out[pool:]
    wide[:, 256:384] = stats

    def spread(target, width):
        def body(b, carry):
            block = wide[pl.ds(pl.multiple_of(b * 8, 8), 8), 0:width]
            for i in range(8):
                target[b * 8 + i] = block[i : i + 1]
            return carry

        lax.fori_loop(0, pool // 8, body, 0)

    spread(part_send, 384)
    part_recv[me] = part_send[me]
    scatter(1, lambda peer: part_send.at[peer], part_recv, "pool", me)

    arrive(1, part_recv, pool)
    parts = part_recv[:, 0, :]
    heads = []
    for j, qj in ((0, q0), (1, q1)):
        maxima = parts[:, 256 + j : 257 + j]
        totals = parts[:, 258 + j : 259 + j]
        new_score = jnp.sum(qj * new_key, axis=1, keepdims=True)
        highest = jnp.maximum(jnp.max(maxima, axis=0, keepdims=True), new_score)
        factor = jnp.exp(maxima - highest)
        new_factor = jnp.exp(new_score - highest)
        weight = jnp.sum(totals * factor, axis=0, keepdims=True) + new_factor
        mixed = jnp.sum(parts[:, 128 * j : 128 * (j + 1)] * factor, axis=0, keepdims=True)
        heads.append((mixed + new_factor * new_value) / weight)
    attended = jnp.concatenate(heads, axis=1).astype(BF16)
    projected = jnp.dot(attended, wo[...], preferred_element_type=F32)
    proj_send[0] = projected
    proj_recv[my_kv] = projected
    scatter(2, lambda peer: proj_send.at[0], proj_recv, "kv", my_kv)
    arrive(2, proj_recv, kv)
    total = proj_recv[0]
    for k in range(1, kv):
        total = total + proj_recv[k]
    residual = rounded(hidden[...].astype(F32) + total)
    mlp_in = rms(residual, mlp_gain).astype(F32)
    groups = mlp_in.shape[1] // LANES
    for g in range(groups):
        in_send[g] = mlp_in[:, g * LANES : (g + 1) * LANES]
    in_recv[me] = in_send[me // 4]
    scatter(3, lambda peer: in_send.at[peer // 4], in_recv, "pool", me)

    arrive(3, in_recv, pool)
    columns = jnp.where(own_lanes, in_recv[:, 0, :], 0.0).astype(BF16)
    half = w_gate.shape[1]
    wide[:, 0:half] = jnp.dot(columns, gate_pad[...], preferred_element_type=F32)
    wide[:, half : 2 * half] = jnp.dot(columns, up_pad[...], preferred_element_type=F32)

    def spread_gu(b):
        at = pl.ds(pl.multiple_of(b * 8, 8), 8)
        gate_rows = wide[at, 0:half]
        up_rows = wide[at, half : 2 * half]
        for i in range(8):
            both = jnp.concatenate([gate_rows[i : i + 1], up_rows[i : i + 1]], axis=0)
            gu_send[b * 8 + i] = both.astype(BF16)

    def send_to(source, target, phase, peer):
        pltpu.make_async_remote_copy(
            src_ref=source,
            dst_ref=target,
            send_sem=send_sem.at[phase],
            recv_sem=recv_sem.at[phase],
            device_id={"pool": peer},
            device_id_type=MESH,
        ).start()

    def along_z(source_of, target, phase):
        for dz in (8, 9, 7, 10, 6, 11, 5, 12, 4, 13, 3, 14, 2, 15, 1):
            z = lax.rem(my_z + dz, 16)
            send_to(source_of(z), target, phase, my_y * 16 + z)

    for dy in (2, 1, 3, 0):
        there = lax.rem(my_y + dy, 4)
        spread_gu(2 * there)
        spread_gu(2 * there + 1)
        if dy:
            send_to(
                gu_send.at[pl.ds(16 * there, 16)], gu_mid.at[my_y], 4, 16 * there + my_z
            )
    gu_mid[my_y] = gu_send[pl.ds(16 * my_y, 16)]
    arrive(4, gu_mid, 4)
    gu_half[...] = jnp.sum(gu_mid[...].astype(F32), axis=0).astype(BF16)
    along_z(lambda z: gu_half.at[z], gu_recv.at[my_z], 8)
    gu_recv[my_z] = gu_half[my_z]
    arrive(8, gu_recv, 16)
    summed = jnp.sum(gu_recv[...].astype(F32), axis=0)
    gate = summed[0:1]
    up = summed[1:2]
    activation = gate / (1.0 + jnp.exp(-gate)) * up
    middle = half // 2
    act_row = jnp.concatenate([activation[:, :middle], activation[:, middle:]], axis=0).astype(BF16)
    act_send[0] = act_row
    along_z(lambda z: act_send.at[0], act_recv.at[my_y, my_z], 5)
    act_recv[my_y, my_z] = act_row
    arrive(5, act_recv.at[0], 16)
    for dy in (2, 1, 3):
        there = lax.rem(my_y + dy, 4)
        send_to(act_recv.at[my_y], act_recv.at[my_y], 9, 16 * there + my_z)

    arrive(9, act_recv, 4)
    activations = act_recv[...].astype(F32).reshape(pool, 2, middle)
    activations = jnp.concatenate([activations[:, 0, :], activations[:, 1, :]], axis=1).astype(BF16)
    down = lax.dot_general(
        activations, down_pad[...], (((1,), (1,)), ((), ())), preferred_element_type=F32
    )
    wide[:, 0:LANES] = jnp.where(own_lanes, down, 0.0)

    spread(down_send, LANES)
    down_recv[me] = down_send[me]
    scatter(6, lambda peer: down_send.at[peer], down_recv, "pool", me)
    arrive(6, down_recv, pool)
    pieces = []
    for g in range(groups):
        piece = down_recv[4 * g]
        for j in range(1, 4):
            piece = piece + down_recv[4 * g + j]
        pieces.append(piece)
    down_row = jnp.concatenate(pieces, axis=1)
    fin_send[0] = down_row
    fin_recv[my_kv] = down_row
    scatter(7, lambda peer: fin_send.at[0], fin_recv, "kv", my_kv)
    arrive(7, fin_recv, kv)
    total = fin_recv[0]
    for k in range(1, kv):
        total = total + fin_recv[k]
    out[...] = (residual + rounded(total)).astype(BF16)

    sent(0, q_recv, pool)
    sent(1, part_recv, pool)
    sent(2, proj_recv, kv)
    sent(3, in_recv, pool)
    sent(4, gu_mid, 4)
    sent(8, gu_recv, 16)
    sent(5, act_recv.at[0], 16)
    sent(9, act_recv, 4)
    sent(6, down_recv, pool)
    sent(7, fin_recv, kv)


def per_device(
    hidden, norm_attn, wq, wkv, wo, cache, slot_entry, lengths, norm_mlp, w_gate, w_up, w_down,
    pool, kv,
):
    width = hidden.shape[1]
    half = w_gate.shape[1]
    tokens = cache.shape[1] * cache.shape[2]
    smem = pl.BlockSpec(memory_space=pltpu.SMEM)
    hbm = pl.BlockSpec(memory_space=pltpu.HBM)
    vmem = pl.BlockSpec(memory_space=pltpu.VMEM)
    return pl.pallas_call(
        functools.partial(layer_kernel, pool, kv),
        out_shape=jax.ShapeDtypeStruct((1, width), BF16),
        in_specs=[smem] * 2 + [hbm] * 10,
        out_specs=vmem,
        scratch_shapes=[
            pltpu.VMEM((1, width), BF16),
            pltpu.VMEM((width // LANES, LANES), BF16),
            pltpu.VMEM((width // LANES, LANES), BF16),
            pltpu.VMEM(wq.shape, BF16),
            pltpu.VMEM(wkv.shape, BF16),
            pltpu.VMEM(wo.shape, BF16),
            pltpu.VMEM((2, tokens, HEAD_SIZE), BF16),
            pltpu.VMEM((pool, 2 * half), F32),
            pltpu.VMEM((LANES, half), BF16),
            pltpu.VMEM((LANES, half), BF16),
            pltpu.VMEM((LANES, half), BF16),
            pltpu.VMEM((1, 1, 256), F32),
            pltpu.VMEM((pool, 1, 256), F32),
            pltpu.VMEM((pool, 1, 384), F32),
            pltpu.VMEM((pool, 1, 384), F32),
            pltpu.VMEM((1, 1, width), F32),
            pltpu.VMEM((kv, 1, width), F32),
            pltpu.VMEM((width // LANES, 1, LANES), F32),
            pltpu.VMEM((pool, 1, LANES), F32),
            pltpu.VMEM((pool, 2, half), BF16),
            pltpu.VMEM((4, 16, 2, half), BF16),
            pltpu.VMEM((16, 2, half), BF16),
            pltpu.VMEM((16, 2, half), BF16),
            pltpu.VMEM((1, 2, half // 2), BF16),
            pltpu.VMEM((4, 16, 2, half // 2), BF16),
            pltpu.VMEM((pool, 1, LANES), F32),
            pltpu.VMEM((pool, 1, LANES), F32),
            pltpu.VMEM((1, 1, width), F32),
            pltpu.VMEM((kv, 1, width), F32),
            pltpu.SemaphoreType.DMA((10,)),
            pltpu.SemaphoreType.DMA((10,)),
            pltpu.SemaphoreType.DMA((19,)),
        ],
        compiler_params=pltpu.CompilerParams(
            collective_id=0, has_side_effects=True, vmem_limit_bytes=67043328
        ),
    )(
        slot_entry, lengths, hidden, norm_attn.reshape(width // LANES, LANES), wq, wkv, wo,
        cache.reshape(2, tokens, HEAD_SIZE), norm_mlp.reshape(width // LANES, LANES),
        w_gate, w_up, w_down.T,
    )


def solution(mesh):
    return jax.shard_map(
        functools.partial(per_device, pool=mesh.shape["pool"], kv=mesh.shape["kv"]),
        mesh=mesh,
        in_specs=(
            P("pool", None),
            P(),
            P(None, "kv"),
            P(None, None, "kv"),
            P("kv", None),
            P(None, "pool", None, "kv"),
            P("pool"),
            P(),
            P(),
            P("pool", "kv"),
            P("pool", "kv"),
            P("kv", "pool"),
        ),
        out_specs=P("pool", None),
        check_vma=False,
    )
```

```python
import functools
import math

import jax
import jax.numpy as jnp
from jax import lax
from jax.experimental import pallas as pl
from jax.experimental.pallas import tpu as pltpu
from jax.sharding import PartitionSpec as P

HEAD_SIZE = 128
LANES = 128
NEGATIVE = -1e30
EPSILON = 1e-05
ROPE_BASE = 1000000.0
MESH = pl.DeviceIdType.MESH
F32 = jnp.float32
BF16 = jnp.bfloat16


def rounded(x):
    return x.astype(BF16).astype(F32)


def rms(x, gain):
    mean_square = jnp.mean(x * x, axis=-1, keepdims=True)
    return (x * lax.rsqrt(mean_square + EPSILON) * gain).astype(BF16)


def turned(angles):
    turns = jnp.floor(angles * (2.0 / math.pi) + 0.5)
    rest = ((angles - turns * 1.5703125) - turns * 4.837512969970703125e-4) - turns * 7.54978995489188216e-8
    square = rest * rest
    sine = rest + rest * square * (
        -1.6666654611e-1 + square * (8.3321608736e-3 - 1.9515295891e-4 * square)
    )
    cosine = 1.0 - 0.5 * square + square * square * (
        4.166664568298827e-2 + square * (-1.388731625493765e-3 + 2.443315711809948e-5 * square)
    )
    quadrant = turns - 4.0 * jnp.floor(turns * 0.25)
    odd = (quadrant == 1.0) | (quadrant == 3.0)
    cos_sign = jnp.where((quadrant == 1.0) | (quadrant == 2.0), -1.0, 1.0)
    sin_sign = jnp.where(quadrant >= 2.0, -1.0, 1.0)
    return jnp.where(odd, sine, cosine) * cos_sign, jnp.where(odd, cosine, sine) * sin_sign


def flat(tile):
    return jnp.concatenate([tile[i : i + 1] for i in range(tile.shape[0])], axis=1)


def layer_kernel(
    pool, kv,
    slot_entry, lengths, hidden_hbm, norm_attn_hbm, wq_hbm, wkv_hbm, wo_hbm, cache_hbm,
    norm_mlp_hbm, w_gate, w_up, w_down,
    out,
    hidden, norm_attn, norm_mlp, wq, wkv, wo, cache,
    wide, gate_pad, up_pad, down_pad,
    q_send, q_recv, part_send, part_recv, proj_send, proj_recv, in_send, in_recv,
    gu_send, gu_mid, gu_half, gu_recv, act_send, act_recv, down_send, down_recv, fin_send, fin_recv,
    send_sem, recv_sem, load_sem,
):
    me = lax.axis_index("pool")
    my_kv = lax.axis_index("kv")
    quarter = lax.rem(me, 4)

    barrier = pltpu.get_barrier_semaphore()

    def greet_pool(k, carry):
        pl.semaphore_signal(
            barrier, inc=1, device_id={"pool": lax.rem(me + k, pool)}, device_id_type=MESH
        )
        return carry

    def greet_kv(k, carry):
        pl.semaphore_signal(
            barrier, inc=1, device_id={"kv": lax.rem(my_kv + k, kv)}, device_id_type=MESH
        )
        return carry

    loads = [
        pltpu.make_async_copy(source, target, load_sem.at[i])
        for i, (source, target) in enumerate(
            [(hidden_hbm, hidden), (norm_attn_hbm, norm_attn), (wq_hbm, wq), (wkv_hbm, wkv),
             (cache_hbm, cache), (wo_hbm, wo), (norm_mlp_hbm, norm_mlp)]
            + [
                (source, target.at[pl.ds(32 * g, 32), :])
                for source, target in ((w_gate, gate_pad), (w_up, up_pad), (w_down, down_pad))
                for g in range(4)
            ]
        )
    ]
    for load in loads[:4]:
        load.start()
    lax.fori_loop(1, pool, greet_pool, 0, unroll=9)
    lax.fori_loop(1, kv, greet_kv, 0, unroll=7)
    for load in loads[4:]:
        load.start()

    my_y = me // 16
    my_z = lax.rem(me, 16)

    def scatter(phase, source_of, target, axis, mine):
        def send(peer):
            pltpu.make_async_remote_copy(
                src_ref=source_of(peer),
                dst_ref=target.at[mine],
                send_sem=send_sem.at[phase],
                recv_sem=recv_sem.at[phase],
                device_id={axis: peer},
                device_id_type=MESH,
            ).start()

        if axis == "kv":
            for k in range(1, kv):
                send(lax.rem(mine + k, kv))
            return

        def at(dy, z):
            send(lax.rem(my_y + dy, 4) * 16 + z)

        def body(t, carry):
            step = (t + 1) // 2
            z = lax.rem(my_z + 24 + (2 * lax.rem(t, 2) - 1) * step, 16)
            for dy in (2, 1, 3, 0):
                at(dy, z)
            return carry

        lax.fori_loop(0, 15, body, 0, unroll=3)
        for dy in (2, 1, 3):
            at(dy, my_z)

    def arrive(phase, target, count):
        view = target.at[pl.ds(0, count - 1)]
        pltpu.make_async_copy(view, view, recv_sem.at[phase]).wait()

    def sent(phase, target, count):
        view = target.at[pl.ds(0, count - 1)]
        pltpu.make_async_copy(view, view, send_sem.at[phase]).wait()

    half_lane = lax.rem(lax.broadcasted_iota(jnp.int32, (1, LANES), 1), HEAD_SIZE // 2)
    frequency = jnp.exp(half_lane.astype(F32) * (-2.0 * math.log(ROPE_BASE) / HEAD_SIZE))
    position = jnp.full((1, LANES), lengths[me], jnp.int32).astype(F32)
    cos_row, sin_row = turned(position * frequency)
    lanes = lax.broadcasted_iota(jnp.int32, (1, LANES), 1)
    sin_row = jnp.where(lanes < HEAD_SIZE // 2, -sin_row, sin_row)
    owned = []
    for i in range(slot_entry.shape[0]):
        entry = slot_entry[i]
        holder_of = jnp.maximum(entry, 0) // 64
        left = lengths[holder_of] - (jnp.maximum(entry, 0) - holder_of * 64) * LANES
        left = jnp.where(entry >= 0, left, 0)
        owned.append(jnp.where(lanes < left, holder_of, -1))
    owner = jnp.concatenate(owned, axis=1)
    loads[0].wait()
    loads[1].wait()
    normed = rms(hidden[...].astype(F32), flat(norm_attn[...].astype(F32)))
    loads[2].wait()
    loads[3].wait()

    def rotated(v):
        return v * cos_row + pltpu.roll(v, HEAD_SIZE // 2, 1) * sin_row

    q = jnp.dot(normed, wq[...], preferred_element_type=F32)
    scale = HEAD_SIZE ** (-0.5)
    q0 = rounded(rotated(q[:, :128]) * scale)
    q1 = rounded(rotated(q[:, 128:]) * scale)
    new_key = rounded(rotated(jnp.dot(normed, wkv[0], preferred_element_type=F32)))
    new_value = rounded(jnp.dot(normed, wkv[1], preferred_element_type=F32))
    own_q = jnp.concatenate([q0, q1], axis=0).astype(BF16)
    q_send[0] = own_q
    q_recv[me] = own_q

    pl.semaphore_wait(barrier, pool - 1 + kv - 1)
    scatter(0, lambda peer: q_send.at[0], q_recv, "pool", me)

    for load in loads[4:]:
        load.wait()
    own_lanes = lax.broadcasted_iota(jnp.int32, (pool, LANES), 1) // 32 == quarter
    mlp_gain = flat(norm_mlp[...].astype(F32))

    arrive(0, q_recv, pool)
    every = q_recv[...].astype(F32)
    rows = jnp.concatenate([every[:, 0, :], every[:, 1, :]], axis=0).astype(BF16)
    scores = lax.dot_general(rows, cache[0], (((1,), (1,)), ((), ())), preferred_element_type=F32)
    row_owner = lax.rem(lax.broadcasted_iota(jnp.int32, (2 * pool, 1), 0), pool)
    taken = row_owner == owner
    scores = jnp.where(taken, scores, NEGATIVE)
    row_max = jnp.max(scores, axis=1, keepdims=True)
    raised = jnp.where(taken, jnp.exp(scores - row_max), 0.0)
    row_total = jnp.sum(raised, axis=1, keepdims=True)
    row_out = jnp.dot(raised.astype(BF16), cache[1], preferred_element_type=F32)
    lane = lax.broadcasted_iota(jnp.int32, (pool, LANES), 1)
    stats = jnp.where(
        lane == 0,
        row_max[:pool],
        jnp.where(lane == 1, row_max[pool:], jnp.where(lane == 2, row_total[:pool], row_total[pool:])),
    )
    wide[:, 0:128] = row_out[:pool]
    wide[:, 128:256] = row_out[pool:]
    wide[:, 256:384] = stats

    def spread(target, width):
        def body(b, carry):
            block = wide[pl.ds(pl.multiple_of(b * 8, 8), 8), 0:width]
            for i in range(8):
                target[b * 8 + i] = block[i : i + 1]
            return carry

        lax.fori_loop(0, pool // 8, body, 0)

    spread(part_send, 384)
    part_recv[me] = part_send[me]
    scatter(1, lambda peer: part_send.at[peer], part_recv, "pool", me)

    arrive(1, part_recv, pool)
    parts = part_recv[:, 0, :]
    heads = []
    for j, qj in ((0, q0), (1, q1)):
        maxima = parts[:, 256 + j : 257 + j]
        totals = parts[:, 258 + j : 259 + j]
        new_score = jnp.sum(qj * new_key, axis=1, keepdims=True)
        highest = jnp.maximum(jnp.max(maxima, axis=0, keepdims=True), new_score)
        factor = jnp.exp(maxima - highest)
        new_factor = jnp.exp(new_score - highest)
        weight = jnp.sum(totals * factor, axis=0, keepdims=True) + new_factor
        mixed = jnp.sum(parts[:, 128 * j : 128 * (j + 1)] * factor, axis=0, keepdims=True)
        heads.append((mixed + new_factor * new_value) / weight)
    attended = jnp.concatenate(heads, axis=1).astype(BF16)
    projected = jnp.dot(attended, wo[...], preferred_element_type=F32)
    proj_send[0] = projected
    proj_recv[my_kv] = projected
    scatter(2, lambda peer: proj_send.at[0], proj_recv, "kv", my_kv)
    arrive(2, proj_recv, kv)
    total = proj_recv[0]
    for k in range(1, kv):
        total = total + proj_recv[k]
    residual = rounded(hidden[...].astype(F32) + total)
    mlp_in = rms(residual, mlp_gain).astype(F32)
    groups = mlp_in.shape[1] // LANES
    for g in range(groups):
        in_send[g] = mlp_in[:, g * LANES : (g + 1) * LANES]
    in_recv[me] = in_send[me // 4]
    scatter(3, lambda peer: in_send.at[peer // 4], in_recv, "pool", me)

    arrive(3, in_recv, pool)
    columns = jnp.where(own_lanes, in_recv[:, 0, :], 0.0).astype(BF16)
    half = w_gate.shape[1]
    wide[:, 0:half] = jnp.dot(columns, gate_pad[...], preferred_element_type=F32)
    wide[:, half : 2 * half] = jnp.dot(columns, up_pad[...], preferred_element_type=F32)

    def spread_gu(b):
        at = pl.ds(pl.multiple_of(b * 8, 8), 8)
        gate_rows = wide[at, 0:half]
        up_rows = wide[at, half : 2 * half]
        for i in range(8):
            both = jnp.concatenate([gate_rows[i : i + 1], up_rows[i : i + 1]], axis=0)
            gu_send[b * 8 + i] = both.astype(BF16)

    def send_to(source, target, phase, peer):
        pltpu.make_async_remote_copy(
            src_ref=source,
            dst_ref=target,
            send_sem=send_sem.at[phase],
            recv_sem=recv_sem.at[phase],
            device_id={"pool": peer},
            device_id_type=MESH,
        ).start()

    def along_z(source_of, target, phase):
        for dz in (8, 9, 7, 10, 6, 11, 5, 12, 4, 13, 3, 14, 2, 15, 1):
            z = lax.rem(my_z + dz, 16)
            send_to(source_of(z), target, phase, my_y * 16 + z)

    for dy in (2, 1, 3, 0):
        there = lax.rem(my_y + dy, 4)
        spread_gu(2 * there)
        spread_gu(2 * there + 1)
        if dy:
            send_to(
                gu_send.at[pl.ds(16 * there, 16)], gu_mid.at[my_y], 4, 16 * there + my_z
            )
    gu_mid[my_y] = gu_send[pl.ds(16 * my_y, 16)]
    arrive(4, gu_mid, 4)
    gu_half[...] = jnp.sum(gu_mid[...].astype(F32), axis=0).astype(BF16)
    along_z(lambda z: gu_half.at[z], gu_recv.at[my_z], 8)
    gu_recv[my_z] = gu_half[my_z]
    arrive(8, gu_recv, 16)
    summed = jnp.sum(gu_recv[...].astype(F32), axis=0)
    gate = summed[0:1]
    up = summed[1:2]
    activation = gate / (1.0 + jnp.exp(-gate)) * up
    middle = half // 2
    act_row = jnp.concatenate([activation[:, :middle], activation[:, middle:]], axis=0).astype(BF16)
    act_send[0] = act_row
    act_recv[me] = act_row
    scatter(5, lambda peer: act_send.at[0], act_recv, "pool", me)

    arrive(5, act_recv, pool)
    activations = act_recv[...].astype(F32)
    activations = jnp.concatenate([activations[:, 0, :], activations[:, 1, :]], axis=1).astype(BF16)
    down = lax.dot_general(
        activations, down_pad[...], (((1,), (1,)), ((), ())), preferred_element_type=F32
    )
    wide[:, 0:LANES] = jnp.where(own_lanes, down, 0.0)

    spread(down_send, LANES)
    down_recv[me] = down_send[me]
    scatter(6, lambda peer: down_send.at[peer], down_recv, "pool", me)
    arrive(6, down_recv, pool)
    pieces = []
    for g in range(groups):
        piece = down_recv[4 * g]
        for j in range(1, 4):
            piece = piece + down_recv[4 * g + j]
        pieces.append(piece)
    down_row = jnp.concatenate(pieces, axis=1)
    fin_send[0] = down_row
    fin_recv[my_kv] = down_row
    scatter(7, lambda peer: fin_send.at[0], fin_recv, "kv", my_kv)
    arrive(7, fin_recv, kv)
    total = fin_recv[0]
    for k in range(1, kv):
        total = total + fin_recv[k]
    out[...] = (residual + rounded(total)).astype(BF16)

    sent(0, q_recv, pool)
    sent(1, part_recv, pool)
    sent(2, proj_recv, kv)
    sent(3, in_recv, pool)
    sent(4, gu_mid, 4)
    sent(8, gu_recv, 16)
    sent(5, act_recv, pool)
    sent(6, down_recv, pool)
    sent(7, fin_recv, kv)


def per_device(
    hidden, norm_attn, wq, wkv, wo, cache, slot_entry, lengths, norm_mlp, w_gate, w_up, w_down,
    pool, kv,
):
    width = hidden.shape[1]
    half = w_gate.shape[1]
    tokens = cache.shape[1] * cache.shape[2]
    smem = pl.BlockSpec(memory_space=pltpu.SMEM)
    hbm = pl.BlockSpec(memory_space=pltpu.HBM)
    vmem = pl.BlockSpec(memory_space=pltpu.VMEM)
    return pl.pallas_call(
        functools.partial(layer_kernel, pool, kv),
        out_shape=jax.ShapeDtypeStruct((1, width), BF16),
        in_specs=[smem] * 2 + [hbm] * 10,
        out_specs=vmem,
        scratch_shapes=[
            pltpu.VMEM((1, width), BF16),
            pltpu.VMEM((width // LANES, LANES), BF16),
            pltpu.VMEM((width // LANES, LANES), BF16),
            pltpu.VMEM(wq.shape, BF16),
            pltpu.VMEM(wkv.shape, BF16),
            pltpu.VMEM(wo.shape, BF16),
            pltpu.VMEM((2, tokens, HEAD_SIZE), BF16),
            pltpu.VMEM((pool, 2 * half), F32),
            pltpu.VMEM((LANES, half), BF16),
            pltpu.VMEM((LANES, half), BF16),
            pltpu.VMEM((LANES, half), BF16),
            pltpu.VMEM((1, 2, HEAD_SIZE), BF16),
            pltpu.VMEM((pool, 2, HEAD_SIZE), BF16),
            pltpu.VMEM((pool, 1, 384), F32),
            pltpu.VMEM((pool, 1, 384), F32),
            pltpu.VMEM((1, 1, width), F32),
            pltpu.VMEM((kv, 1, width), F32),
            pltpu.VMEM((width // LANES, 1, LANES), F32),
            pltpu.VMEM((pool, 1, LANES), F32),
            pltpu.VMEM((pool, 2, half), BF16),
            pltpu.VMEM((4, 16, 2, half), BF16),
            pltpu.VMEM((16, 2, half), BF16),
            pltpu.VMEM((16, 2, half), BF16),
            pltpu.VMEM((1, 2, half // 2), BF16),
            pltpu.VMEM((pool, 2, half // 2), BF16),
            pltpu.VMEM((pool, 1, LANES), F32),
            pltpu.VMEM((pool, 1, LANES), F32),
            pltpu.VMEM((1, 1, width), F32),
            pltpu.VMEM((kv, 1, width), F32),
            pltpu.SemaphoreType.DMA((9,)),
            pltpu.SemaphoreType.DMA((9,)),
            pltpu.SemaphoreType.DMA((19,)),
        ],
        compiler_params=pltpu.CompilerParams(
            collective_id=0, has_side_effects=True, vmem_limit_bytes=67043328
        ),
    )(
        slot_entry, lengths, hidden, norm_attn.reshape(width // LANES, LANES), wq, wkv, wo,
        cache.reshape(2, tokens, HEAD_SIZE), norm_mlp.reshape(width // LANES, LANES),
        w_gate, w_up, w_down.T,
    )


def solution(mesh):
    return jax.shard_map(
        functools.partial(per_device, pool=mesh.shape["pool"], kv=mesh.shape["kv"]),
        mesh=mesh,
        in_specs=(
            P("pool", None),
            P(),
            P(None, "kv"),
            P(None, None, "kv"),
            P("kv", None),
            P(None, "pool", None, "kv"),
            P("pool"),
            P(),
            P(),
            P("pool", "kv"),
            P("pool", "kv"),
            P("kv", "pool"),
        ),
        out_specs=P("pool", None),
        check_vma=False,
    )
```

```python
import functools
import math

import jax
import jax.numpy as jnp
from jax import lax
from jax.experimental import pallas as pl
from jax.experimental.pallas import tpu as pltpu
from jax.sharding import PartitionSpec as P

HEAD_SIZE = 128
LANES = 128
NEGATIVE = -1e30
EPSILON = 1e-05
ROPE_BASE = 1000000.0
MESH = pl.DeviceIdType.MESH
F32 = jnp.float32
BF16 = jnp.bfloat16


def rounded(x):
    return x.astype(BF16).astype(F32)


def rms(x, gain):
    mean_square = jnp.mean(x * x, axis=-1, keepdims=True)
    return (x * lax.rsqrt(mean_square + EPSILON) * gain).astype(BF16)


def turned(angles):
    turns = jnp.floor(angles * (2.0 / math.pi) + 0.5)
    rest = ((angles - turns * 1.5703125) - turns * 4.837512969970703125e-4) - turns * 7.54978995489188216e-8
    square = rest * rest
    sine = rest + rest * square * (
        -1.6666654611e-1 + square * (8.3321608736e-3 - 1.9515295891e-4 * square)
    )
    cosine = 1.0 - 0.5 * square + square * square * (
        4.166664568298827e-2 + square * (-1.388731625493765e-3 + 2.443315711809948e-5 * square)
    )
    quadrant = turns - 4.0 * jnp.floor(turns * 0.25)
    odd = (quadrant == 1.0) | (quadrant == 3.0)
    cos_sign = jnp.where((quadrant == 1.0) | (quadrant == 2.0), -1.0, 1.0)
    sin_sign = jnp.where(quadrant >= 2.0, -1.0, 1.0)
    return jnp.where(odd, sine, cosine) * cos_sign, jnp.where(odd, cosine, sine) * sin_sign


def flat(tile):
    return jnp.concatenate([tile[i : i + 1] for i in range(tile.shape[0])], axis=1)


def layer_kernel(
    pool, kv,
    slot_entry, lengths, hidden_hbm, norm_attn_hbm, wq_hbm, wkv_hbm, wo_hbm, cache_hbm,
    norm_mlp_hbm, w_gate, w_up, w_down,
    out,
    hidden, norm_attn, norm_mlp, wq, wkv, wo, cache,
    wide, gate_pad, up_pad, down_pad,
    q_send, q_recv, part_send, part_recv, proj_send, proj_recv, in_send, in_recv,
    gu_send, gu_mid, gu_half, gu_recv, act_send, act_recv, down_send, down_recv, fin_send, fin_recv,
    send_sem, recv_sem, load_sem,
):
    me = lax.axis_index("pool")
    my_kv = lax.axis_index("kv")
    quarter = lax.rem(me, 4)

    barrier = pltpu.get_barrier_semaphore()

    my_y = me // 16
    my_z = lax.rem(me, 16)

    def far_z(t):
        return lax.rem(my_z + 24 + (2 * lax.rem(t, 2) - 1) * ((t + 1) // 2), 16)

    def greet(dy, z):
        pl.semaphore_signal(
            barrier, inc=1, device_id={"pool": lax.rem(my_y + dy, 4) * 16 + z}, device_id_type=MESH
        )

    def greet_far(t, carry):
        z = far_z(t)
        for dy in (2, 1, 3, 0):
            greet(dy, z)
        return carry

    lax.fori_loop(0, 15, greet_far, 0, unroll=3)
    for dy in (2, 1, 3):
        greet(dy, my_z)
    for k in range(1, kv):
        pl.semaphore_signal(
            barrier, inc=1, device_id={"kv": lax.rem(my_kv + k, kv)}, device_id_type=MESH
        )

    loads = [
        pltpu.make_async_copy(source, target, load_sem.at[i])
        for i, (source, target) in enumerate(
            [(hidden_hbm, hidden), (norm_attn_hbm, norm_attn), (wq_hbm, wq), (wkv_hbm, wkv),
             (cache_hbm, cache), (wo_hbm, wo), (norm_mlp_hbm, norm_mlp)]
            + [
                (source, target.at[pl.ds(32 * g, 32), :])
                for source, target in ((w_gate, gate_pad), (w_up, up_pad), (w_down, down_pad))
                for g in range(4)
            ]
        )
    ]
    for load in loads:
        load.start()

    def scatter(phase, source_of, target, axis, mine):
        def send(peer):
            pltpu.make_async_remote_copy(
                src_ref=source_of(peer),
                dst_ref=target.at[mine],
                send_sem=send_sem.at[phase],
                recv_sem=recv_sem.at[phase],
                device_id={axis: peer},
                device_id_type=MESH,
            ).start()

        if axis == "kv":
            for k in range(1, kv):
                send(lax.rem(mine + k, kv))
            return

        def at(dy, z):
            send(lax.rem(my_y + dy, 4) * 16 + z)

        def body(t, carry):
            z = far_z(t)
            for dy in (2, 1, 3, 0):
                at(dy, z)
            return carry

        lax.fori_loop(0, 15, body, 0, unroll=3)
        for dy in (2, 1, 3):
            at(dy, my_z)

    def arrive(phase, target, count):
        view = target.at[pl.ds(0, count - 1)]
        pltpu.make_async_copy(view, view, recv_sem.at[phase]).wait()

    def sent(phase, target, count):
        view = target.at[pl.ds(0, count - 1)]
        pltpu.make_async_copy(view, view, send_sem.at[phase]).wait()

    half_lane = lax.rem(lax.broadcasted_iota(jnp.int32, (1, LANES), 1), HEAD_SIZE // 2)
    frequency = jnp.exp(half_lane.astype(F32) * (-2.0 * math.log(ROPE_BASE) / HEAD_SIZE))
    position = jnp.full((1, LANES), lengths[me], jnp.int32).astype(F32)
    cos_row, sin_row = turned(position * frequency)
    lanes = lax.broadcasted_iota(jnp.int32, (1, LANES), 1)
    sin_row = jnp.where(lanes < HEAD_SIZE // 2, -sin_row, sin_row)
    owned = []
    for i in range(slot_entry.shape[0]):
        entry = slot_entry[i]
        holder_of = jnp.maximum(entry, 0) // 64
        left = lengths[holder_of] - (jnp.maximum(entry, 0) - holder_of * 64) * LANES
        left = jnp.where(entry >= 0, left, 0)
        owned.append(jnp.where(lanes < left, holder_of, -1))
    owner = jnp.concatenate(owned, axis=1)
    loads[0].wait()
    loads[1].wait()
    normed = rms(hidden[...].astype(F32), flat(norm_attn[...].astype(F32)))
    loads[2].wait()
    loads[3].wait()

    def rotated(v):
        return v * cos_row + pltpu.roll(v, HEAD_SIZE // 2, 1) * sin_row

    q = jnp.dot(normed, wq[...], preferred_element_type=F32)
    scale = HEAD_SIZE ** (-0.5)
    q0 = rounded(rotated(q[:, :128]) * scale)
    q1 = rounded(rotated(q[:, 128:]) * scale)
    new_key = rounded(rotated(jnp.dot(normed, wkv[0], preferred_element_type=F32)))
    new_value = rounded(jnp.dot(normed, wkv[1], preferred_element_type=F32))
    own_q = jnp.concatenate([q0, q1], axis=0).astype(BF16)
    q_send[0] = own_q
    q_recv[me] = own_q

    pl.semaphore_wait(barrier, pool - 1 + kv - 1)
    scatter(0, lambda peer: q_send.at[0], q_recv, "pool", me)

    for load in loads[4:]:
        load.wait()
    own_lanes = lax.broadcasted_iota(jnp.int32, (pool, LANES), 1) // 32 == quarter
    mlp_gain = flat(norm_mlp[...].astype(F32))

    arrive(0, q_recv, pool)
    every = q_recv[...].astype(F32)
    rows = jnp.concatenate([every[:, 0, :], every[:, 1, :]], axis=0).astype(BF16)
    scores = lax.dot_general(rows, cache[0], (((1,), (1,)), ((), ())), preferred_element_type=F32)
    row_owner = lax.rem(lax.broadcasted_iota(jnp.int32, (2 * pool, 1), 0), pool)
    taken = row_owner == owner
    scores = jnp.where(taken, scores, NEGATIVE)
    row_max = jnp.max(scores, axis=1, keepdims=True)
    raised = jnp.where(taken, jnp.exp(scores - row_max), 0.0)
    row_total = jnp.sum(raised, axis=1, keepdims=True)
    row_out = jnp.dot(raised.astype(BF16), cache[1], preferred_element_type=F32)
    lane = lax.broadcasted_iota(jnp.int32, (pool, LANES), 1)
    stats = jnp.where(
        lane == 0,
        row_max[:pool],
        jnp.where(lane == 1, row_max[pool:], jnp.where(lane == 2, row_total[:pool], row_total[pool:])),
    )
    wide[:, 0:128] = row_out[:pool]
    wide[:, 128:256] = row_out[pool:]
    wide[:, 256:384] = stats

    def spread(target, width):
        def body(b, carry):
            block = wide[pl.ds(pl.multiple_of(b * 8, 8), 8), 0:width]
            for i in range(8):
                target[b * 8 + i] = block[i : i + 1]
            return carry

        lax.fori_loop(0, pool // 8, body, 0)

    spread(part_send, 384)
    part_recv[me] = part_send[me]
    scatter(1, lambda peer: part_send.at[peer], part_recv, "pool", me)

    arrive(1, part_recv, pool)
    parts = part_recv[:, 0, :]
    heads = []
    for j, qj in ((0, q0), (1, q1)):
        maxima = parts[:, 256 + j : 257 + j]
        totals = parts[:, 258 + j : 259 + j]
        new_score = jnp.sum(qj * new_key, axis=1, keepdims=True)
        highest = jnp.maximum(jnp.max(maxima, axis=0, keepdims=True), new_score)
        factor = jnp.exp(maxima - highest)
        new_factor = jnp.exp(new_score - highest)
        weight = jnp.sum(totals * factor, axis=0, keepdims=True) + new_factor
        mixed = jnp.sum(parts[:, 128 * j : 128 * (j + 1)] * factor, axis=0, keepdims=True)
        heads.append((mixed + new_factor * new_value) / weight)
    attended = jnp.concatenate(heads, axis=1).astype(BF16)
    projected = jnp.dot(attended, wo[...], preferred_element_type=F32)
    proj_send[0] = projected
    proj_recv[my_kv] = projected
    scatter(2, lambda peer: proj_send.at[0], proj_recv, "kv", my_kv)
    arrive(2, proj_recv, kv)
    total = proj_recv[0]
    for k in range(1, kv):
        total = total + proj_recv[k]
    residual = rounded(hidden[...].astype(F32) + total)
    mlp_in = rms(residual, mlp_gain).astype(F32)
    groups = mlp_in.shape[1] // LANES
    for g in range(groups):
        in_send[g] = mlp_in[:, g * LANES : (g + 1) * LANES]
    in_recv[me] = in_send[me // 4]
    scatter(3, lambda peer: in_send.at[peer // 4], in_recv, "pool", me)

    arrive(3, in_recv, pool)
    columns = jnp.where(own_lanes, in_recv[:, 0, :], 0.0).astype(BF16)
    half = w_gate.shape[1]
    wide[:, 0:half] = jnp.dot(columns, gate_pad[...], preferred_element_type=F32)
    wide[:, half : 2 * half] = jnp.dot(columns, up_pad[...], preferred_element_type=F32)

    def spread_gu(b):
        at = pl.ds(pl.multiple_of(b * 8, 8), 8)
        gate_rows = wide[at, 0:half]
        up_rows = wide[at, half : 2 * half]
        for i in range(8):
            both = jnp.concatenate([gate_rows[i : i + 1], up_rows[i : i + 1]], axis=0)
            gu_send[b * 8 + i] = both.astype(BF16)

    def send_to(source, target, phase, peer):
        pltpu.make_async_remote_copy(
            src_ref=source,
            dst_ref=target,
            send_sem=send_sem.at[phase],
            recv_sem=recv_sem.at[phase],
            device_id={"pool": peer},
            device_id_type=MESH,
        ).start()

    def along_z(source_of, target, phase):
        for dz in (8, 9, 7, 10, 6, 11, 5, 12, 4, 13, 3, 14, 2, 15, 1):
            z = lax.rem(my_z + dz, 16)
            send_to(source_of(z), target, phase, my_y * 16 + z)

    for dy in (2, 1, 3, 0):
        there = lax.rem(my_y + dy, 4)
        spread_gu(2 * there)
        spread_gu(2 * there + 1)
        if dy:
            send_to(
                gu_send.at[pl.ds(16 * there, 16)], gu_mid.at[my_y], 4, 16 * there + my_z
            )
    gu_mid[my_y] = gu_send[pl.ds(16 * my_y, 16)]
    arrive(4, gu_mid, 4)
    gu_half[...] = jnp.sum(gu_mid[...].astype(F32), axis=0).astype(BF16)
    along_z(lambda z: gu_half.at[z], gu_recv.at[my_z], 8)
    gu_recv[my_z] = gu_half[my_z]
    arrive(8, gu_recv, 16)
    summed = jnp.sum(gu_recv[...].astype(F32), axis=0)
    gate = summed[0:1]
    up = summed[1:2]
    activation = gate / (1.0 + jnp.exp(-gate)) * up
    middle = half // 2
    act_row = jnp.concatenate([activation[:, :middle], activation[:, middle:]], axis=0).astype(BF16)
    act_send[0] = act_row
    act_recv[me] = act_row
    scatter(5, lambda peer: act_send.at[0], act_recv, "pool", me)

    arrive(5, act_recv, pool)
    activations = act_recv[...].astype(F32)
    activations = jnp.concatenate([activations[:, 0, :], activations[:, 1, :]], axis=1).astype(BF16)
    down = lax.dot_general(
        activations, down_pad[...], (((1,), (1,)), ((), ())), preferred_element_type=F32
    )
    wide[:, 0:LANES] = jnp.where(own_lanes, down, 0.0)

    spread(down_send, LANES)
    down_recv[me] = down_send[me]
    scatter(6, lambda peer: down_send.at[peer], down_recv, "pool", me)
    arrive(6, down_recv, pool)
    pieces = []
    for g in range(groups):
        piece = down_recv[4 * g]
        for j in range(1, 4):
            piece = piece + down_recv[4 * g + j]
        pieces.append(piece)
    down_row = jnp.concatenate(pieces, axis=1)
    fin_send[0] = down_row
    fin_recv[my_kv] = down_row
    scatter(7, lambda peer: fin_send.at[0], fin_recv, "kv", my_kv)
    arrive(7, fin_recv, kv)
    total = fin_recv[0]
    for k in range(1, kv):
        total = total + fin_recv[k]
    out[...] = (residual + rounded(total)).astype(BF16)

    sent(0, q_recv, pool)
    sent(1, part_recv, pool)
    sent(2, proj_recv, kv)
    sent(3, in_recv, pool)
    sent(4, gu_mid, 4)
    sent(8, gu_recv, 16)
    sent(5, act_recv, pool)
    sent(6, down_recv, pool)
    sent(7, fin_recv, kv)


def per_device(
    hidden, norm_attn, wq, wkv, wo, cache, slot_entry, lengths, norm_mlp, w_gate, w_up, w_down,
    pool, kv,
):
    width = hidden.shape[1]
    half = w_gate.shape[1]
    tokens = cache.shape[1] * cache.shape[2]
    smem = pl.BlockSpec(memory_space=pltpu.SMEM)
    hbm = pl.BlockSpec(memory_space=pltpu.HBM)
    vmem = pl.BlockSpec(memory_space=pltpu.VMEM)
    return pl.pallas_call(
        functools.partial(layer_kernel, pool, kv),
        out_shape=jax.ShapeDtypeStruct((1, width), BF16),
        in_specs=[smem] * 2 + [hbm] * 10,
        out_specs=vmem,
        scratch_shapes=[
            pltpu.VMEM((1, width), BF16),
            pltpu.VMEM((width // LANES, LANES), BF16),
            pltpu.VMEM((width // LANES, LANES), BF16),
            pltpu.VMEM(wq.shape, BF16),
            pltpu.VMEM(wkv.shape, BF16),
            pltpu.VMEM(wo.shape, BF16),
            pltpu.VMEM((2, tokens, HEAD_SIZE), BF16),
            pltpu.VMEM((pool, 2 * half), F32),
            pltpu.VMEM((LANES, half), BF16),
            pltpu.VMEM((LANES, half), BF16),
            pltpu.VMEM((LANES, half), BF16),
            pltpu.VMEM((1, 2, HEAD_SIZE), BF16),
            pltpu.VMEM((pool, 2, HEAD_SIZE), BF16),
            pltpu.VMEM((pool, 1, 384), F32),
            pltpu.VMEM((pool, 1, 384), F32),
            pltpu.VMEM((1, 1, width), F32),
            pltpu.VMEM((kv, 1, width), F32),
            pltpu.VMEM((width // LANES, 1, LANES), F32),
            pltpu.VMEM((pool, 1, LANES), F32),
            pltpu.VMEM((pool, 2, half), BF16),
            pltpu.VMEM((4, 16, 2, half), BF16),
            pltpu.VMEM((16, 2, half), BF16),
            pltpu.VMEM((16, 2, half), BF16),
            pltpu.VMEM((1, 2, half // 2), BF16),
            pltpu.VMEM((pool, 2, half // 2), BF16),
            pltpu.VMEM((pool, 1, LANES), F32),
            pltpu.VMEM((pool, 1, LANES), F32),
            pltpu.VMEM((1, 1, width), F32),
            pltpu.VMEM((kv, 1, width), F32),
            pltpu.SemaphoreType.DMA((9,)),
            pltpu.SemaphoreType.DMA((9,)),
            pltpu.SemaphoreType.DMA((19,)),
        ],
        compiler_params=pltpu.CompilerParams(
            collective_id=0, has_side_effects=True, vmem_limit_bytes=67043328
        ),
    )(
        slot_entry, lengths, hidden, norm_attn.reshape(width // LANES, LANES), wq, wkv, wo,
        cache.reshape(2, tokens, HEAD_SIZE), norm_mlp.reshape(width // LANES, LANES),
        w_gate, w_up, w_down.T,
    )


def solution(mesh):
    return jax.shard_map(
        functools.partial(per_device, pool=mesh.shape["pool"], kv=mesh.shape["kv"]),
        mesh=mesh,
        in_specs=(
            P("pool", None),
            P(),
            P(None, "kv"),
            P(None, None, "kv"),
            P("kv", None),
            P(None, "pool", None, "kv"),
            P("pool"),
            P(),
            P(),
            P("pool", "kv"),
            P("pool", "kv"),
            P("kv", "pool"),
        ),
        out_specs=P("pool", None),
        check_vma=False,
    )
```
